32 devices in a mesh: groups: 2 (over y), seg: 4 (over z), section: 4 (over x, core).
Axes of the slice: x: 2, y: 2, z: 4, core: 2. Of those that a mesh axis runs over, the one named last changes fastest.
Arguments:
- writes: bfloat16 [8, 128, 2048], P(('groups', 'seg'), None, 'section'), parts along dimension 0, may hold values from -6 to 6
- layer_inputs: bfloat16 [4, 8, 256, 2048], P('section', ('groups', 'seg')), parts along dimension 1, may hold values from -6 to 6
- upstream: bfloat16 [4, 8, 256, 2048], P('section', ('groups', 'seg')), parts along dimension 1, may hold values from -6 to 6
- pattern: int32 [8, 2, 3], P(('groups', 'seg')), parts along dimension 0, may hold values 0 or 1
- w_q: bfloat16 [4, 2048, 1024], P('section', 'seg'), may hold values from -0.125 to 0.125
- w_kv: bfloat16 [4, 2048, 512], P('section', 'seg'), may hold values from -0.125 to 0.125
- w_o: bfloat16 [4, 1024, 2048], P('section', 'seg'), may hold values from -0.1875 to 0.1875
- norm_gain: float32 [4, 2048], P('section'), may hold values from 0.5 to 10
- gate_weight: float32 [4, 2048, 16], P('section'), may hold values from -0.125 to 0.125
- gate_bias: float32 [4, 16], P('section'), may hold values from -2 to 6
Outputs:
- section_grads: bfloat16 [4, 8, 256, 2048], P('section', ('groups', 'seg')), parts along dimension 1
- memory_grads: bfloat16 [4, 8, 128, 2048], P('section', ('groups', 'seg')), parts along dimension 1
The draws below stay inside these ranges and needn't reach their ends.
There are 2 independent parts, one for each index of `groups`. The reference program is written for one: setup_inputs(seed, part) draws one part's arguments, and reference() takes and returns one part's arrays. A program takes and returns all parts, laid end to end along the dimension named above; an argument that names none is the same for every part. Nothing has to cross between parts.
All inputs are finite; a program needn't handle non-finite values. No bound on the sum of `pattern` on one device may be relied on, other than what follows from the above.
Results may differ from the reference program's by a relative error of at most 0.03.
The reference program's roundings to bfloat16 on the way count: a program that leaves them out, or rounds other values in their place, can miss the bound.
Values may be sent and summed in bfloat16 or wider, within the bound.
A program may use at most 128 MiB of HBM per device.

```python
import jax
import jax.numpy as jnp
from jax import lax

D = 2048
HEADS = 16
KV_HEADS = 4
HEAD = 64
BLK = 128
MEM = 128
SEG_LEN = 256
SEGMENTS = 4
N_SECTION = 4


def draw_norm_gain(key, part):
    values = jnp.clip(1.0 + 0.1 * jax.random.normal(key, (N_SECTION, D), jnp.float32), 0.5, 1.5)
    return values


def with_ends(values, rng, least, high):
    longest = values.shape.index(max(values.shape))
    spots = []
    for shift in (0, 1):
        where = [jax.random.randint(jax.random.fold_in(rng, axis), (), 0, length) for axis, length in enumerate(values.shape)]
        where[longest] = (where[longest] + shift) % values.shape[longest]
        spots.append(tuple(where))
    return values.at[spots[0]].set(least).at[spots[1]].set(high)


def block_levels(rng, dims, pieces, least, high):
    level, own = 1.0, jax.random.fold_in(rng, 6)
    for axis_at, blocks in pieces:
        heights = jnp.exp(jax.random.uniform(jax.random.fold_in(own, axis_at), (blocks,), jnp.float32, least / len(pieces), high / len(pieces)))
        level = level * jnp.repeat(heights, dims[axis_at] // blocks).reshape([-1 if axis == axis_at else 1 for axis in range(len(dims))])
    return level


def bell_draw(key, dims, deviation, bound, split=(), kind=jnp.bfloat16):
    array = deviation * jax.random.normal(key, dims, jnp.float32)
    if split:
        array = array * block_levels(key, dims, split, -0.22, 0.18)
    return jnp.clip(array, -bound, bound).astype(kind)


def setup_inputs(seed: int = 0, part: int = 0) -> dict:
    arg_keys = jax.random.split(jax.random.key(seed), 11)
    own_keys = jax.random.split(jax.random.fold_in(arg_keys[10], part), 11)
    return {
        "writes": bell_draw(own_keys[0], (SEGMENTS, MEM, D), 1.0, 6.0, ((0, 4), (2, 4))),
        "layer_inputs": bell_draw(own_keys[1], (N_SECTION, SEGMENTS, SEG_LEN, D), 1.0, 6.0, ((0, 4), (1, 4))),
        "upstream": bell_draw(own_keys[2], (N_SECTION, SEGMENTS, SEG_LEN, D), 1.0, 6.0, ((0, 4), (1, 4))),
        "pattern": with_ends((jax.random.randint(own_keys[3], (SEGMENTS, SEG_LEN // BLK, SEG_LEN // BLK + 1), 0, 2) < 1).astype(jnp.int32), jax.random.fold_in(own_keys[3], 1), 0, 1),
        "w_q": bell_draw(arg_keys[4], (N_SECTION, D, HEADS * HEAD), D ** -0.5, 0.125, ((0, 4), (1, 4))),
        "w_kv": bell_draw(arg_keys[5], (N_SECTION, D, 2 * KV_HEADS * HEAD), D ** -0.5, 0.125, ((0, 4), (1, 4))),
        "w_o": bell_draw(arg_keys[6], (N_SECTION, HEADS * HEAD, D), (HEADS * HEAD) ** -0.5, 0.1875, ((0, 4), (1, 4))),
        "norm_gain": draw_norm_gain(jax.random.fold_in(arg_keys[10], 71), part),
        "gate_weight": bell_draw(arg_keys[8], (N_SECTION, D, HEADS), D ** -0.5, 0.125, ((0, 4),), jnp.float32),
        "gate_bias": jnp.clip(-2.0 + 8.0 * jax.random.uniform(arg_keys[9], (N_SECTION, HEADS), jnp.float32) ** block_levels(arg_keys[9], (N_SECTION, HEADS), ((0, 4),), -0.2, 0.2), -2.0, 6.0),
    }


epsilon = 1e-05
masked_score = -1e+30

def normed_rows(values, gain):
    widened = values.astype(jnp.float32)
    scale = lax.rsqrt(lax.optimization_barrier(jnp.mean(widened * widened, axis=-1, keepdims=True)) + epsilon)
    return (widened * scale * gain).astype(jnp.bfloat16)

def allowed_keys(positions, layout, block_rows, memory_rows, total_rows):
    blocks = layout.shape[0]
    query_block = positions // block_rows
    chooser = (query_block[:, None] == jnp.arange(blocks, dtype=jnp.int32)[None, :]).astype(jnp.int32)
    picked = lax.optimization_barrier(jnp.sum(chooser[:, :, None] * layout[None, :, :], axis=1))
    token_index = jnp.arange(total_rows, dtype=jnp.int32)
    key_block = token_index // block_rows
    spread = (key_block[None, :] == jnp.arange(blocks, dtype=jnp.int32)[:, None]).astype(jnp.int32)
    token_pattern = lax.optimization_barrier(jnp.sum(picked[:, 1:, None] * spread[None, :, :], axis=1))
    earlier = (key_block[None, :] < query_block[:, None]) & (token_pattern > 0)
    causal = (key_block[None, :] == query_block[:, None]) & (token_index[None, :] <= positions[:, None])
    memory_part = jnp.broadcast_to((picked[:, 0] > 0)[:, None], (positions.shape[0], memory_rows))
    return jnp.concatenate([memory_part, earlier | causal], axis=1)

def attend_rows(queries, keyvals, allowed):
    count = queries.shape[0]
    sources = keyvals.shape[0]
    grouped = queries.astype(jnp.float32).reshape(count, KV_HEADS, HEADS // KV_HEADS, HEAD)
    keys = keyvals[:, :KV_HEADS * HEAD].astype(jnp.float32).reshape(sources, KV_HEADS, HEAD)
    values = keyvals[:, KV_HEADS * HEAD:].astype(jnp.float32).reshape(sources, KV_HEADS, HEAD)
    scores = jnp.einsum('qgre,sge->grqs', grouped, keys) * HEAD ** (-0.5)
    scores = jnp.where(allowed[None, None], scores, masked_score)
    peak = lax.stop_gradient(lax.optimization_barrier(jnp.max(scores, axis=-1, keepdims=True)))
    weights = jnp.exp(scores - peak)
    probs = (weights / lax.optimization_barrier(jnp.sum(weights, axis=-1, keepdims=True))).astype(jnp.bfloat16)
    mixed = jnp.einsum('grqs,sge->qgre', probs.astype(jnp.float32), values)
    return mixed.reshape(count, HEADS * HEAD).astype(jnp.bfloat16)

def apply_layer(stream, memory, layout, query_weight, pair_weight, out_weight, gain):
    memory_rows = memory.shape[0]
    count = stream.shape[0]
    normed = normed_rows(jnp.concatenate([memory, stream], axis=0), gain)
    queries = jnp.dot(normed[memory_rows:], query_weight, preferred_element_type=jnp.float32).astype(jnp.bfloat16)
    keyvals = jnp.dot(normed, pair_weight, preferred_element_type=jnp.float32).astype(jnp.bfloat16)
    positions = jnp.arange(count, dtype=jnp.int32)
    allowed = allowed_keys(positions, layout, BLK, memory_rows, count)
    mixed = attend_rows(queries, keyvals, allowed)
    added = jnp.dot(mixed, out_weight, preferred_element_type=jnp.float32)
    return (stream.astype(jnp.float32) + added).astype(jnp.bfloat16)

def memory_states(writes, gate_weight, gate_bias):
    widened = writes.astype(jnp.float32)
    logits = jnp.einsum('smd,dg->smg', widened, gate_weight, precision=lax.Precision.HIGHEST) + gate_bias
    keep = jax.nn.sigmoid(logits)
    segments, rows, width = widened.shape
    grouped = widened.reshape(segments, rows, HEADS, width // HEADS)

    def advance(state, item):
        keep_now, write_now = item
        following = keep_now[:, :, None] * state + (1.0 - keep_now)[:, :, None] * write_now
        return (following, state)
    start = jnp.zeros((rows, HEADS, width // HEADS), jnp.float32)
    _, states = lax.scan(advance, start, (keep, grouped))
    return states.reshape(segments, rows, width).astype(jnp.bfloat16)

def reference(writes, layer_inputs, upstream, pattern, w_q, w_kv, w_o, norm_gain, gate_weight, gate_bias):
    section_list = []
    memory_list = []
    for level in range(N_SECTION):
        memory = memory_states(writes, gate_weight[level], gate_bias[level])

        def backward_one(item, level=level):
            rows_in, memory_in, layout, incoming = item

            def mapping(first_arg, second_arg):
                return apply_layer(first_arg, second_arg, layout, w_q[level], w_kv[level], w_o[level], norm_gain[level])
            _, pull = jax.vjp(mapping, rows_in, memory_in)
            return pull(incoming)
        grad_rows, grad_memory = lax.map(backward_one, (layer_inputs[level], memory, pattern, upstream[level]))
        section_list.append(grad_rows.astype(jnp.bfloat16))
        memory_list.append(grad_memory.astype(jnp.bfloat16))
    return (jnp.stack(section_list), jnp.stack(memory_list))
```

```python
import functools

import jax
import jax.numpy as jnp
from jax import lax
from jax.experimental import pallas as pl
from jax.experimental.pallas import tpu as pltpu
from jax.sharding import PartitionSpec as P

HEADS = 16
KV_HEADS = 4
HEAD = 64
BLK = 128
MEM = 128


epsilon = 1e-05
masked_score = -1e30
GROUP = HEADS // KV_HEADS
NT = (((1,), (1,)), ((), ()))
TN = (((0,), (0,)), ((), ()))
CHUNKS = KV_HEADS
PAIR = 2
STRIPS = 4
Q0 = PAIR
O0 = PAIR + CHUNKS
ITEMS = PAIR + CHUNKS + STRIPS
MESH = pl.DeviceIdType.MESH


def layer_kernel(
    n,
    groups,
    sections,
    pattern,
    writes,
    rows_far,
    up_far,
    gain,
    gate,
    gate_bias,
    w_kv,
    w_q,
    w_o,
    grad_rows,
    grad_memory,
    rows_in,
    ups,
    all_writes,
    all_kv,
    all_q,
    all_o,
    normed,
    scales,
    memory,
    state,
    passed,
    gates,
    keys,
    values,
    bias,
    dmixed,
    dmixed_out,
    dq,
    dkeys,
    dvalues,
    rowdots,
    *sems,
):
    (
        up_sem,
        down_sem,
        zrecv,
        xsend,
        xrecv,
        ysend,
        yrecv,
        wsend,
        wrecv,
        psend,
        precv,
        usend,
        urecv,
        dsend,
        drecv,
        local,
    ) = sems
    g = lax.axis_index("groups")
    s = lax.axis_index("seg")
    c = lax.axis_index("section")
    count, width = rows_in.shape
    wide = writes.shape[1]
    span = all_q.shape[1] // CHUNKS
    half_kv = all_kv.shape[1] // PAIR
    f32, bf16 = jnp.float32, jnp.bfloat16
    native = n == CHUNKS

    owner = lax.rem(c, groups)
    owns = g == owner
    first, last = s == 0, s == n - 1
    end = first | last
    inner = jnp.logical_not(end)
    near_end = (s == 1) | (s == n - 2)
    far = jnp.where(s == 1, 0, n - 1)
    inward = jnp.where(first, 1, n - 2)

    def lanes(at, size):
        return pl.ds(pl.multiple_of(at * size, size), size)

    mine = lanes(c, wide)

    barrier = pltpu.get_barrier_semaphore()

    def greet(where):
        pl.semaphore_signal(barrier, inc=1, device_id=where, device_id_type=MESH)

    @pl.when(s > 0)
    def _():
        greet((g, s - 1, c))

    @pl.when(s < n - 1)
    def _():
        greet((g, s + 1, c))

    for d in range(1, groups):
        greet((lax.rem(g + d, groups), s, c))

        @pl.when(end)
        def _():
            greet((lax.rem(g + d, groups), inward, c))

        @pl.when(near_end)
        def _():
            greet((lax.rem(g + d, groups), far, c))

    for d in range(1, sections):
        greet((g, s, lax.rem(c + d, sections)))

    def input_copy(k):
        if k == 0:
            return pltpu.make_async_copy(rows_far, rows_in, local.at[3])
        return pltpu.make_async_copy(up_far, ups.at[g], local.at[4])

    input_copy(0).start()
    input_copy(1).start()

    beside = jnp.where(end, 1, 2) + jnp.where(end | near_end, groups - 1, 0)
    pl.semaphore_wait(barrier, beside + groups + sections - 2)

    def remote(src, dst, send, recv, where):
        return pltpu.make_async_remote_copy(
            src_ref=src,
            dst_ref=dst,
            send_sem=send,
            recv_sem=recv,
            device_id=where,
            device_id_type=MESH,
        )

    def operand(i):
        if i < Q0:
            return w_kv, all_kv, half_kv, i
        if i < O0:
            return w_q, all_q, span, i - Q0
        return w_o, all_o, width // STRIPS, i - O0

    def spot(i, shard, part):
        src, dst, cols, chunk = operand(i)
        at = slice(chunk * cols, (chunk + 1) * cols)
        if i >= O0:
            return dst.at[lanes(shard, src.shape[0]), at]
        half = src.shape[0] // groups
        return dst.at[lanes(shard * groups + part, half), at]

    def source(i, part):
        src, dst, cols, chunk = operand(i)
        at = slice(chunk * cols, (chunk + 1) * cols)
        if i >= O0:
            return src.at[:, at]
        return src.at[lanes(part, src.shape[0] // groups), at]

    def up(i, shard, own=False):
        there = spot(i, shard, g)
        src = source(i, g) if own else there
        return remote(src, there, up_sem.at[i, shard], zrecv.at[i, shard], (g, s + 1, c))

    def down(i, shard, own=False):
        there = spot(i, shard, g)
        src = source(i, g) if own else there
        return remote(src, there, down_sem.at[i, shard], zrecv.at[i, shard], (g, s - 1, c))

    def extra(j, d, shard, own=False):
        part = lax.rem(g + d, groups)
        there = spot(Q0 + j, shard, part)
        src = source(Q0 + j, part) if own else there
        return remote(src, there, xsend.at[j, d], xrecv.at[j, d], (g, inward, c))

    def across(i, shard, d, part):
        there = spot(i, shard, part)
        return remote(
            there,
            there,
            ysend.at[i, shard, d],
            yrecv.at[i, shard, d],
            (lax.rem(g + d, groups), s, c),
        )

    def write_up(shard, own=False):
        there = all_writes.at[shard, :, mine]
        return remote(
            writes if own else there, there, wsend.at[shard], wrecv.at[shard], (g, s + 1, c)
        )

    def write_peer(shard, d, origin):
        there = all_writes.at[shard, :, lanes(origin, wide)]
        return remote(
            there,
            there,
            psend.at[shard, d],
            precv.at[shard, d],
            (g, s, lax.rem(c + d, sections)),
        )

    def pull_near():
        return remote(up_far, ups.at[g], usend.at[0], urecv.at[g], (owner, s, c))

    def pull_far():
        at = groups + g
        return remote(up_far, ups.at[at], usend.at[0], urecv.at[at], (owner, inward, c))

    def give_back(j, u, where):
        return remote(
            dmixed_out.at[j, u],
            dmixed.at[j],
            dsend.at[j, u],
            drecv.at[j],
            (lax.rem(u, groups), where, c),
        )

    def own_copy(w):
        src, dst = ((w_kv, all_kv), (w_o, all_o), (w_q, all_q))[w]
        return pltpu.make_async_copy(src, dst.at[lanes(s, src.shape[0]), :], local.at[w])

    def rises(i):
        return (owns & (s > 0) & (s < n - 2)) | (owns & first) if i >= O0 else s < n - 1

    def falls(i):
        return (owns & (s < n - 1) & (s > 1)) | (owns & last) if i >= O0 else s > 0

    def skips(i, shard):
        if i < Q0:
            return False
        return ((shard == 0) & (s == 1)) | ((shard == n - 1) & (s == n - 2))

    def start_own(i):
        @pl.when(rises(i))
        def _():
            up(i, s, True).start()

        @pl.when(falls(i))
        def _():
            down(i, s, True).start()

    def spread(i, shard):
        if i >= O0:
            return
        if i < Q0:
            for d in range(1, groups):
                across(i, shard, d, g).start()
        else:

            @pl.when(jnp.logical_not(skips(i, shard)))
            def _():
                for d in range(1, groups):
                    across(i, shard, d, g).start()

    def from_below(i, shard):
        up(i, shard).wait_recv()

        @pl.when(rises(i))
        def _():
            up(i, shard).start()

        spread(i, shard)

    def from_above(i, shard):
        down(i, shard).wait_recv()

        @pl.when(falls(i))
        def _():
            down(i, shard).start()

        spread(i, shard)

    def reaches(i):
        return owns & inner if i >= O0 else True

    def serve(i, k, inside=False):
        low = 1 if inside else 0

        @pl.when((s - k >= low) & reaches(i))
        def _():
            from_below(i, s - k)

        @pl.when((s + k < n - low) & reaches(i))
        def _():
            from_above(i, s + k)

    def serve_ends(j):
        @pl.when(s > 0)
        def _():
            from_below(Q0 + j, 0)

        @pl.when(s < n - 1)
        def _():
            from_above(Q0 + j, n - 1)

    def finish(i):
        @pl.loop(0, n)
        def _(shard):
            skipped = skips(i, shard)

            @pl.when((shard != s) & jnp.logical_not(skipped))
            def _():
                for d in range(1, groups):
                    across(i, shard, d, lax.rem(g + groups - d, groups)).wait_recv()

            if i >= Q0:

                @pl.when(skipped)
                def _():
                    for d in range(1, groups):
                        extra(i - Q0, d, shard).wait_recv()

    def drain(i):
        @pl.loop(0, n)
        def _(shard):
            if i < O0:

                @pl.when((shard != s) & jnp.logical_not(skips(i, shard)))
                def _():
                    for d in range(1, groups):
                        across(i, shard, d, g).wait_send()

            below = (shard <= s) & rises(i)
            above = (shard >= s) & falls(i)

            @pl.when(below)
            def _():
                up(i, shard).wait_send()

            @pl.when(above)
            def _():
                down(i, shard).wait_send()

    @pl.when(s < n - 1)
    def _():
        write_up(s, True).start()

    for i in range(PAIR):
        start_own(i)

    @pl.when(inner & jnp.logical_not(owns))
    def _():
        pull_near().start()

    for i in range(O0, ITEMS):
        start_own(i)

    @pl.when(end)
    def _():
        pull_far().start()

    for j in range(CHUNKS):
        start_own(Q0 + j)

    @pl.when(end)
    def _():
        for j in range(CHUNKS):
            for d in range(1, groups):
                extra(j, d, s, True).start()

    for w in range(3):
        own_copy(w).start()

    strip = 32

    def norm_rows(from_ref, to_row):
        @pl.loop(0, from_ref.shape[0] // strip)
        def _(r):
            x = from_ref[lanes(r, strip), :].astype(f32)
            scale = lax.rsqrt(jnp.mean(x * x, axis=-1, keepdims=True) + epsilon)
            to = pl.ds(pl.multiple_of(to_row + r * strip, strip), strip)
            normed[to, :] = (x * scale * gain[...]).astype(bf16)
            scales[to, :] = scale

    input_copy(0).wait()
    input_copy(1).wait()
    norm_rows(rows_in, MEM)

    whole_gate = gate[...]
    high = whole_gate.astype(bf16)
    rest = whole_gate - high.astype(f32)
    middle = rest.astype(bf16)
    gates[0] = high
    gates[1] = middle
    gates[2] = (rest - middle.astype(f32)).astype(bf16)

    keyed = lax.broadcasted_iota(jnp.int32, (BLK, BLK), 0)
    asked = lax.broadcasted_iota(jnp.int32, (BLK, BLK), 1)
    blocks = count // BLK
    for b in range(blocks):
        to = slice(b * BLK, (b + 1) * BLK)
        seen = jnp.where(pattern[b, 0] > 0, 0.0, masked_score)
        bias[:MEM, to] = jnp.full((MEM, BLK), seen, f32)
        for e in range(blocks):
            where = slice(MEM + e * BLK, MEM + (e + 1) * BLK)
            if e == b:
                bias[where, to] = jnp.where(keyed <= asked, 0.0, masked_score).astype(f32)
            elif e < b:
                seen = jnp.where(pattern[b, 1 + e] > 0, 0.0, masked_score)
                bias[where, to] = jnp.full((BLK, BLK), seen, f32)
            else:
                bias[where, to] = jnp.full((BLK, BLK), masked_score, f32)

    state[...] = jnp.zeros_like(state)
    passed[...] = jnp.ones_like(passed)
    cut = width // HEADS

    def serve_writes(k):
        @pl.when(s - k >= 0)
        def _():
            write_up(s - k).wait_recv()

            @pl.when(s < n - 1)
            def _():
                write_up(s - k).start()

            for d in range(1, sections):
                write_peer(s - k, d, c).start()

    def add_writes(k):
        @pl.when(s - k >= 0)
        def _():
            for d in range(1, sections):
                write_peer(s - k, d, lax.rem(c + sections - d, sections)).wait_recv()
            w = all_writes[s - k]
            logits = sum(
                lax.dot_general(w, gates[p], NT, preferred_element_type=f32) for p in range(3)
            )
            keep = jax.nn.sigmoid(logits + gate_bias[...])
            fresh = passed[...] * (1.0 - keep)
            passed[...] = passed[...] * keep
            for h in range(HEADS):
                at = slice(h * cut, (h + 1) * cut)
                state[:, at] += fresh[:, h : h + 1] * w[:, at].astype(f32)

    def project(t):
        j = jnp.where(s < n // 2, t, CHUNKS - 1 - t)
        weight = all_o[lanes(j, span), :]

        @pl.loop(0, 2 * groups)
        def _(u):
            @pl.when((u < groups) | near_end)
            def _():
                part = lax.dot_general(
                    ups[u], weight, NT, preferred_element_type=f32
                ).astype(bf16)

                @pl.when(u == g)
                def _():
                    dmixed[j] = part

                @pl.when(u != g)
                def _():
                    dmixed_out[j, u] = part

                @pl.when((u < groups) & (u != g))
                def _():
                    give_back(j, u, s).start()

                @pl.when((u >= groups) & sent_far(j))
                def _():
                    give_back(j, u, far).start()

    def sent_far(j):
        return (j != far) if native else (j >= 0)

    def wait_pulls():
        own_copy(1).wait()

        @pl.loop(0, 2 * groups)
        def _(u):
            @pl.when(((u < groups) | near_end) & (u != g))
            def _():
                remote(up_far, ups.at[u], usend.at[0], urecv.at[u], beyond).wait_recv()

    beyond = (lax.rem(g + 1, groups), s, c)

    serve_writes(1)
    for i in range(PAIR):
        serve(i, 1)
    for i in range(O0, ITEMS):
        serve(i, 1)
    for j in range(CHUNKS):
        serve(Q0 + j, 1, True)
    add_writes(1)

    if n == 4:
        serve_writes(2)
        for i in range(PAIR):
            serve(i, 2)
        for j in range(CHUNKS):
            serve(Q0 + j, 2, True)

        @pl.when(owns & inner)
        def _():
            wait_pulls()
            for t in range(3):
                project(t)

        for i in range(O0, ITEMS):
            serve(i, 2)

        @pl.when(owns & inner)
        def _():
            project(3)

        add_writes(2)
        serve_writes(3)
        for i in range(PAIR):
            serve(i, 3)
        add_writes(3)
    else:

        @pl.loop(2, n)
        def _(k):
            serve_writes(k)
            for i in range(PAIR):
                serve(i, k)
            for i in range(O0, ITEMS):
                serve(i, k)
            for j in range(CHUNKS):
                serve(Q0 + j, k, True)
            add_writes(k)

        @pl.when(owns & inner)
        def _():
            wait_pulls()
            for t in range(CHUNKS):
                project(t)

    @pl.when(jnp.logical_not(owns & inner))
    def _():
        own_copy(1).wait()

        if native:

            @pl.when(end)
            def _():
                dmixed[s] = lax.dot_general(
                    ups[g], all_o[lanes(s, span), :], NT, preferred_element_type=f32
                ).astype(bf16)

    memory[...] = state[...].astype(bf16)
    norm_rows(memory, 0)

    own_copy(0).wait()
    own_copy(2).wait()
    for i in range(PAIR):
        finish(i)
    for kind, to in ((0, keys), (1, values)):
        part = jnp.dot(
            normed[...], all_kv[:, kind * span : (kind + 1) * span], preferred_element_type=f32
        ).astype(bf16)
        for h in range(KV_HEADS):
            to[h] = part[:, h * HEAD : (h + 1) * HEAD]

    rowdots[...] = jnp.zeros_like(rowdots)

    def attend(j):
        ready = owns & inner
        if native:
            ready = ready | (end & (j == s))

        @pl.when(jnp.logical_not(ready))
        def _():
            remote(
                dmixed_out.at[j, 0], dmixed.at[j], dsend.at[j, 0], drecv.at[j], beyond
            ).wait_recv()

        queries = jnp.dot(
            normed[MEM:, :], all_q[:, lanes(j, span)], preferred_element_type=f32
        ).astype(bf16)
        small = (queries.astype(f32) * HEAD ** (-0.5)).astype(bf16)
        key, value = keys[j], values[j]
        small_key = (key.astype(f32) * HEAD ** (-0.5)).astype(bf16)
        pulled = dmixed[j]
        dkey = jnp.zeros(key.shape, f32)
        dvalue = jnp.zeros(value.shape, f32)
        dquery = []
        for h in range(GROUP):
            at = slice(h * HEAD, (h + 1) * HEAD)
            query, dhead = small[:, at], pulled[:, at]
            scores = lax.dot_general(key, query, NT, preferred_element_type=f32) + bias[...]
            raised = jnp.exp(scores - jnp.max(scores, axis=0, keepdims=True))
            probs = raised * (1.0 / jnp.sum(raised, axis=0, keepdims=True))
            dprobs = lax.dot_general(value, dhead, NT, preferred_element_type=f32)
            drop = jnp.sum(probs * dprobs, axis=0, keepdims=True)
            dscores = (probs * (dprobs - drop)).astype(bf16)
            dvalue += jnp.dot(probs.astype(bf16), dhead, preferred_element_type=f32)
            dkey += jnp.dot(dscores, query, preferred_element_type=f32)
            dquery.append(lax.dot_general(small_key, dscores, TN, preferred_element_type=f32))
        dkey = dkey.astype(bf16)
        dvalue = dvalue.astype(bf16)
        dkeys[j] = dkey
        dvalues[j] = dvalue
        dquery = jnp.concatenate(dquery, axis=0).T.astype(bf16)
        dq[:, lanes(j, span)] = dquery
        rowdots[...] += jnp.sum(
            dkey.astype(f32) * key.astype(f32) + dvalue.astype(f32) * value.astype(f32),
            axis=-1,
            keepdims=True,
        )
        rowdots[MEM:, :] += jnp.sum(
            dquery.astype(f32) * queries.astype(f32), axis=-1, keepdims=True
        )

    serve_ends(0)
    for j in range(CHUNKS):
        if j < CHUNKS - 1:
            serve_ends(j + 1)
        finish(Q0 + j)
        attend(j)

    dkv = jnp.concatenate(
        [dkeys[h] for h in range(KV_HEADS)] + [dvalues[h] for h in range(KV_HEADS)], axis=1
    )
    tile = 256
    scale = scales[...]
    coef = rowdots[...] * scale * scale * (1.0 / width)

    @pl.loop(0, width // tile)
    def _(t):
        at = lanes(t, tile)
        both = lax.dot_general(dkv, all_kv[at, :], NT, preferred_element_type=f32)
        ones = lax.dot_general(dq[...], all_q[at, :], NT, preferred_element_type=f32)
        strength = gain[:, at]
        grad_memory[:, at] = (
            both[:MEM] * strength * scale[:MEM] - memory[:, at].astype(f32) * coef[:MEM]
        ).astype(bf16)
        grad_rows[:, at] = (
            (both[MEM:] + ones) * strength * scale[MEM:]
            - rows_in[:, at].astype(f32) * coef[MEM:]
            + ups[g, :, at].astype(f32)
        ).astype(bf16)

    @pl.loop(0, n)
    def _(shard):
        @pl.when(shard < s)
        def _():
            for d in range(1, sections):
                write_peer(shard, d, c).wait_send()

        @pl.when((shard <= s) & (s < n - 1))
        def _():
            write_up(shard).wait_send()

    for i in range(ITEMS):
        drain(i)

    @pl.when(end)
    def _():
        pull_far().wait_send()
        for j in range(CHUNKS):
            for d in range(1, groups):
                extra(j, d, s, True).wait_send()

    @pl.when(inner & jnp.logical_not(owns))
    def _():
        pull_near().wait_send()

    @pl.when(inner & owns)
    def _():
        @pl.loop(0, CHUNKS)
        def _(j):
            @pl.loop(0, 2 * groups)
            def _(u):
                @pl.when((u < groups) & (u != g))
                def _():
                    give_back(j, u, s).wait_send()

                @pl.when((u >= groups) & near_end & sent_far(j))
                def _():
                    give_back(j, u, far).wait_send()


def per_device(
    n,
    groups,
    sections,
    writes,
    layer_inputs,
    upstream,
    pattern,
    w_q,
    w_kv,
    w_o,
    norm_gain,
    gate_weight,
    gate_bias,
):
    count, width = layer_inputs.shape[2:]
    total = MEM + count
    span = HEADS * HEAD // CHUNKS
    anywhere = pl.BlockSpec(memory_space=pl.ANY)
    near = pl.BlockSpec(memory_space=pltpu.VMEM)
    dma = pltpu.SemaphoreType.DMA
    bf16, f32 = jnp.bfloat16, jnp.float32
    grads = pl.pallas_call(
        functools.partial(layer_kernel, n, groups, sections),
        out_shape=[
            jax.ShapeDtypeStruct((count, width), bf16),
            jax.ShapeDtypeStruct((MEM, width), bf16),
        ],
        in_specs=[pl.BlockSpec(memory_space=pltpu.SMEM), anywhere, anywhere, anywhere]
        + [near] * 3
        + [anywhere] * 3,
        out_specs=[near, near],
        scratch_shapes=[
            pltpu.VMEM((count, width), bf16),
            pltpu.VMEM((2 * groups, count, width), bf16),
            pltpu.VMEM((n, MEM, width), bf16),
            pltpu.VMEM((width, w_kv.shape[2]), bf16),
            pltpu.VMEM((width, HEADS * HEAD), bf16),
            pltpu.VMEM((HEADS * HEAD, width), bf16),
            pltpu.VMEM((total, width), bf16),
            pltpu.VMEM((total, 1), f32),
            pltpu.VMEM((MEM, width), bf16),
            pltpu.VMEM((MEM, width), f32),
            pltpu.VMEM((MEM, HEADS), f32),
            pltpu.VMEM((3, HEADS, width), bf16),
            pltpu.VMEM((KV_HEADS, total, HEAD), bf16),
            pltpu.VMEM((KV_HEADS, total, HEAD), bf16),
            pltpu.VMEM((total, count), f32),
            pltpu.VMEM((KV_HEADS, count, span), bf16),
            pltpu.VMEM((KV_HEADS, 2 * groups, count, span), bf16),
            pltpu.VMEM((count, HEADS * HEAD), bf16),
            pltpu.VMEM((KV_HEADS, total, HEAD), bf16),
            pltpu.VMEM((KV_HEADS, total, HEAD), bf16),
            pltpu.VMEM((total, 1), f32),
            dma((ITEMS, n)),
            dma((ITEMS, n)),
            dma((ITEMS, n)),
            dma((CHUNKS, groups)),
            dma((CHUNKS, groups)),
            dma((O0, n, groups)),
            dma((O0, n, groups)),
            dma((n,)),
            dma((n,)),
            dma((n, sections)),
            dma((n, sections)),
            dma((1,)),
            dma((2 * groups,)),
            dma((CHUNKS, 2 * groups)),
            dma((CHUNKS,)),
            dma((5,)),
        ],
        compiler_params=pltpu.CompilerParams(
            collective_id=0, has_side_effects=True, vmem_limit_bytes=56 * 1024 * 1024
        ),
    )(
        pattern[0],
        writes[0],
        layer_inputs[0, 0],
        upstream[0, 0],
        norm_gain,
        gate_weight[0].T,
        gate_bias,
        w_kv[0],
        w_q[0],
        w_o[0],
    )
    return (grads[0][None, None], grads[1][None, None])


def solution(mesh):
    placed = (
        P(("groups", "seg"), None, "section"),
        P("section", ("groups", "seg"), None, None),
        P("section", ("groups", "seg"), None, None),
        P(("groups", "seg"), None, None),
        P("section", "seg", None),
        P("section", "seg", None),
        P("section", "seg", None),
        P("section", None),
        P("section", None, None),
        P("section", None),
    )
    sizes = (mesh.shape["seg"], mesh.shape["groups"], mesh.shape["section"])
    return jax.shard_map(
        functools.partial(per_device, *sizes),
        mesh=mesh,
        in_specs=placed,
        out_specs=(
            P("section", ("groups", "seg"), None, None),
            P("section", ("groups", "seg"), None, None),
        ),
        check_vma=False,
    )
```

```python
import functools

import jax
import jax.numpy as jnp
from jax import lax
from jax.experimental import pallas as pl
from jax.experimental.pallas import tpu as pltpu
from jax.sharding import PartitionSpec as P

HEADS = 16
KV_HEADS = 4
HEAD = 64
BLK = 128
MEM = 128


epsilon = 1e-05
masked_score = -1e30
GROUP = HEADS // KV_HEADS
NT = (((1,), (1,)), ((), ()))
TN = (((0,), (0,)), ((), ()))
CHUNKS = KV_HEADS
PAIR = 2
STRIPS = 4
KV, Q, O = 0, PAIR, PAIR + CHUNKS
PIECES = {KV: PAIR, Q: CHUNKS, O: STRIPS}
ITEMS = PAIR + CHUNKS + STRIPS
MESH = pl.DeviceIdType.MESH


def layer_kernel(
    n,
    groups,
    sections,
    pattern,
    writes,
    rows_far,
    up_far,
    gain,
    gate,
    gate_bias,
    w_kv,
    w_q,
    w_o,
    grad_rows,
    grad_memory,
    rows_in,
    ups,
    all_writes,
    all_kv,
    all_q,
    all_o,
    normed,
    scales,
    memory,
    state,
    passed,
    gates,
    keys,
    values,
    bias,
    dmixed,
    dmixed_out,
    dq,
    dkeys,
    dvalues,
    rowdots,
    *sems,
):
    (
        up_sem,
        down_sem,
        zrecv,
        xsend,
        xrecv,
        ysend,
        yrecv,
        wsend,
        wrecv,
        psend,
        precv,
        usend,
        urecv,
        dsend,
        drecv,
        local,
    ) = sems
    g = lax.axis_index("groups")
    s = lax.axis_index("seg")
    c = lax.axis_index("section")
    count, width = rows_in.shape
    wide = writes.shape[1]
    span = all_q.shape[1] // CHUNKS
    half_kv = all_kv.shape[1] // PAIR
    f32, bf16 = jnp.float32, jnp.bfloat16
    native = n == CHUNKS

    owner = lax.rem(c, groups)
    owns = g == owner
    first, last = s == 0, s == n - 1
    end = first | last
    inner = jnp.logical_not(end)
    near_end = (s == 1) | (s == n - 2)
    far = jnp.where(s == 1, 0, n - 1)
    inward = jnp.where(first, 1, n - 2)

    def lanes(at, size):
        return pl.ds(pl.multiple_of(at * size, size), size)

    mine = lanes(c, wide)

    barrier = pltpu.get_barrier_semaphore()

    def greet(where):
        pl.semaphore_signal(barrier, inc=1, device_id=where, device_id_type=MESH)

    @pl.when(s > 0)
    def _():
        greet((g, s - 1, c))

    @pl.when(s < n - 1)
    def _():
        greet((g, s + 1, c))

    for d in range(1, groups):
        greet((lax.rem(g + d, groups), s, c))

        @pl.when(end)
        def _():
            greet((lax.rem(g + d, groups), inward, c))

        @pl.when(near_end)
        def _():
            greet((lax.rem(g + d, groups), far, c))

    for d in range(1, sections):
        greet((g, s, lax.rem(c + d, sections)))

    def input_copy(k):
        if k == 0:
            return pltpu.make_async_copy(rows_far, rows_in, local.at[3])
        return pltpu.make_async_copy(up_far, ups.at[g], local.at[4])

    input_copy(0).start()
    input_copy(1).start()

    beside = jnp.where(end, 1, 2) + jnp.where(end | near_end, groups - 1, 0)
    pl.semaphore_wait(barrier, beside + groups + sections - 2)

    def remote(src, dst, send, recv, where):
        return pltpu.make_async_remote_copy(
            src_ref=src,
            dst_ref=dst,
            send_sem=send,
            recv_sem=recv,
            device_id=where,
            device_id_type=MESH,
        )

    def operand(kind):
        return {
            KV: (w_kv, all_kv, half_kv),
            Q: (w_q, all_q, span),
            O: (w_o, all_o, width // STRIPS),
        }[kind]

    def columns(kind, chunk):
        cols = operand(kind)[2]
        if isinstance(chunk, int):
            return slice(chunk * cols, (chunk + 1) * cols)
        return lanes(chunk, cols)

    def spot(item, shard, part):
        kind, chunk = item
        src, dst, _ = operand(kind)
        at = columns(kind, chunk)
        if kind == O:
            return dst.at[lanes(shard, src.shape[0]), at]
        half = src.shape[0] // groups
        return dst.at[lanes(shard * groups + part, half), at]

    def source(item, part):
        kind, chunk = item
        src = operand(kind)[0]
        at = columns(kind, chunk)
        if kind == O:
            return src.at[:, at]
        return src.at[lanes(part, src.shape[0] // groups), at]

    def up(item, shard, own=False):
        i, there = item[0] + item[1], spot(item, shard, g)
        src = source(item, g) if own else there
        return remote(src, there, up_sem.at[i, shard], zrecv.at[i, shard], (g, s + 1, c))

    def down(item, shard, own=False):
        i, there = item[0] + item[1], spot(item, shard, g)
        src = source(item, g) if own else there
        return remote(src, there, down_sem.at[i, shard], zrecv.at[i, shard], (g, s - 1, c))

    def extra(j, d, shard, own=False):
        part = lax.rem(g + d, groups)
        there = spot((Q, j), shard, part)
        src = source((Q, j), part) if own else there
        return remote(src, there, xsend.at[j, d], xrecv.at[j, d], (g, inward, c))

    def across(item, shard, d, part):
        i, there = item[0] + item[1], spot(item, shard, part)
        return remote(
            there,
            there,
            ysend.at[i, shard, d],
            yrecv.at[i, shard, d],
            (lax.rem(g + d, groups), s, c),
        )

    def write_up(shard, own=False):
        there = all_writes.at[shard, :, mine]
        return remote(
            writes if own else there, there, wsend.at[shard], wrecv.at[shard], (g, s + 1, c)
        )

    def write_peer(shard, d, origin):
        there = all_writes.at[shard, :, lanes(origin, wide)]
        return remote(
            there,
            there,
            psend.at[shard, d],
            precv.at[shard, d],
            (g, s, lax.rem(c + d, sections)),
        )

    def pull_near():
        return remote(up_far, ups.at[g], usend.at[0], urecv.at[g], (owner, s, c))

    def pull_far():
        at = groups + g
        return remote(up_far, ups.at[at], usend.at[0], urecv.at[at], (owner, inward, c))

    def give_back(j, u, where):
        return remote(
            dmixed_out.at[j, u],
            dmixed.at[j],
            dsend.at[j, u],
            drecv.at[j],
            (lax.rem(u, groups), where, c),
        )

    def own_copy(w):
        src, dst = ((w_kv, all_kv), (w_o, all_o), (w_q, all_q))[w]
        return pltpu.make_async_copy(src, dst.at[lanes(s, src.shape[0]), :], local.at[w])

    def rises(kind):
        return (owns & (s > 0) & (s < n - 2)) | (owns & first) if kind == O else s < n - 1

    def falls(kind):
        return (owns & (s < n - 1) & (s > 1)) | (owns & last) if kind == O else s > 0

    def skips(kind, shard):
        if kind != Q:
            return shard < 0
        return ((shard == 0) & (s == 1)) | ((shard == n - 1) & (s == n - 2))

    def pieces(kind):
        return [(kind, k) for k in range(PIECES[kind])]

    rising = list(reversed(pieces(Q)))

    def start_own(kind):
        for fall in pieces(kind):
            rise = (kind, CHUNKS - 1 - fall[1]) if kind == Q else fall

            @pl.when(rises(kind))
            def _():
                up(rise, s, True).start()

            @pl.when(falls(kind))
            def _():
                down(fall, s, True).start()

    def spread(item, shard):
        if item[0] == O:
            return

        def send():
            for d in range(1, groups):
                across(item, shard, d, g).start()

        if item[0] == KV:
            send()
        else:
            pl.when(jnp.logical_not(skips(Q, shard)))(send)

    def from_below(item, shard):
        up(item, shard).wait_recv()

        @pl.when(rises(item[0]))
        def _():
            up(item, shard).start()

        spread(item, shard)

    def from_above(item, shard):
        down(item, shard).wait_recv()

        @pl.when(falls(item[0]))
        def _():
            down(item, shard).start()

        spread(item, shard)

    def reaches(kind):
        return owns & inner if kind == O else s >= 0

    def serve(kind, k, inside=False):
        low = 1 if inside else 0

        @pl.when((s - k >= low) & reaches(kind))
        def _():
            for item in rising if kind == Q else pieces(kind):
                from_below(item, s - k)

        @pl.when((s + k < n - low) & reaches(kind))
        def _():
            for item in pieces(kind):
                from_above(item, s + k)

    def finish(item):
        @pl.loop(0, n)
        def _(shard):
            skipped = skips(item[0], shard)

            @pl.when((shard != s) & jnp.logical_not(skipped))
            def _():
                for d in range(1, groups):
                    across(item, shard, d, lax.rem(g + groups - d, groups)).wait_recv()

            if item[0] == Q:

                @pl.when(skipped)
                def _():
                    for d in range(1, groups):
                        extra(item[1], d, shard).wait_recv()

    def drain(item):
        kind = item[0]

        @pl.loop(0, n)
        def _(shard):
            if kind != O:

                @pl.when((shard != s) & jnp.logical_not(skips(kind, shard)))
                def _():
                    for d in range(1, groups):
                        across(item, shard, d, g).wait_send()

            @pl.when((shard <= s) & rises(kind))
            def _():
                up(item, shard).wait_send()

            @pl.when((shard >= s) & falls(kind))
            def _():
                down(item, shard).wait_send()

    @pl.when(s < n - 1)
    def _():
        write_up(s, True).start()

    start_own(KV)

    @pl.when(inner & jnp.logical_not(owns))
    def _():
        pull_near().start()

    start_own(O)
    start_own(Q)

    @pl.when(end)
    def _():
        pull_far().start()

    for w in range(3):
        own_copy(w).start()

    strip = 32

    def norm_rows(from_ref, to_row):
        @pl.loop(0, from_ref.shape[0] // strip)
        def _(r):
            x = from_ref[lanes(r, strip), :].astype(f32)
            scale = lax.rsqrt(jnp.mean(x * x, axis=-1, keepdims=True) + epsilon)
            to = pl.ds(pl.multiple_of(to_row + r * strip, strip), strip)
            normed[to, :] = (x * scale * gain[...]).astype(bf16)
            scales[to, :] = scale

    input_copy(0).wait()
    input_copy(1).wait()
    norm_rows(rows_in, MEM)

    whole_gate = gate[...]
    high = whole_gate.astype(bf16)
    rest = whole_gate - high.astype(f32)
    middle = rest.astype(bf16)
    gates[0] = high
    gates[1] = middle
    gates[2] = (rest - middle.astype(f32)).astype(bf16)

    keyed = lax.broadcasted_iota(jnp.int32, (BLK, BLK), 0)
    asked = lax.broadcasted_iota(jnp.int32, (BLK, BLK), 1)
    blocks = count // BLK
    for b in range(blocks):
        to = slice(b * BLK, (b + 1) * BLK)
        seen = jnp.where(pattern[b, 0] > 0, 0.0, masked_score)
        bias[:MEM, to] = jnp.full((MEM, BLK), seen, f32)
        for e in range(blocks):
            where = slice(MEM + e * BLK, MEM + (e + 1) * BLK)
            if e == b:
                bias[where, to] = jnp.where(keyed <= asked, 0.0, masked_score).astype(f32)
            elif e < b:
                seen = jnp.where(pattern[b, 1 + e] > 0, 0.0, masked_score)
                bias[where, to] = jnp.full((BLK, BLK), seen, f32)
            else:
                bias[where, to] = jnp.full((BLK, BLK), masked_score, f32)

    state[...] = jnp.zeros_like(state)
    passed[...] = jnp.ones_like(passed)
    cut = width // HEADS

    def serve_writes(k):
        @pl.when(s - k >= 0)
        def _():
            write_up(s - k).wait_recv()

            @pl.when(s < n - 1)
            def _():
                write_up(s - k).start()

            for d in range(1, sections):
                write_peer(s - k, d, c).start()

    def add_writes(k):
        @pl.when(s - k >= 0)
        def _():
            for d in range(1, sections):
                write_peer(s - k, d, lax.rem(c + sections - d, sections)).wait_recv()
            w = all_writes[s - k]
            logits = sum(
                lax.dot_general(w, gates[p], NT, preferred_element_type=f32) for p in range(3)
            )
            keep = jax.nn.sigmoid(logits + gate_bias[...])
            fresh = passed[...] * (1.0 - keep)
            passed[...] = passed[...] * keep
            for h in range(HEADS):
                at = slice(h * cut, (h + 1) * cut)
                state[:, at] += fresh[:, h : h + 1] * w[:, at].astype(f32)

    def turn(t):
        return jnp.where(s < n // 2, t, CHUNKS - 1 - t)

    def sent_far(j):
        return (j != far) if native else (j >= 0)

    def give_all(t, away):
        j = turn(t)
        base = groups if away else 0
        weight = all_o[lanes(j, span), :]
        pulled = ups[base : base + groups].reshape(groups * count, width)
        part = lax.dot_general(pulled, weight, NT, preferred_element_type=f32).astype(bf16)
        for u in range(groups):
            piece = part[u * count : (u + 1) * count]
            dmixed_out[j, base + u] = piece
            if away:

                @pl.when(sent_far(j))
                def _():
                    give_back(j, base + u, far).start()

            else:

                @pl.when(u == g)
                def _():
                    dmixed[j] = piece

                @pl.when(u != g)
                def _():
                    give_back(j, u, s).start()

    def project(t):
        pl.when(owns & inner)(lambda: give_all(t, False))

    def project_far(t):
        pl.when(owns & near_end)(lambda: give_all(t, True))

    beyond = (lax.rem(g + 1, groups), s, c)

    def wait_pulls(low, high):
        @pl.loop(low, high)
        def _(u):
            @pl.when(u != g)
            def _():
                remote(up_far, ups.at[u], usend.at[0], urecv.at[u], beyond).wait_recv()

    def ready_near():
        @pl.when(owns & inner)
        def _():
            own_copy(1).wait()
            wait_pulls(0, groups)

    def ready_far():
        @pl.when(owns & near_end)
        def _():
            wait_pulls(groups, 2 * groups)

    def start_extras():
        @pl.when(end)
        def _():
            for j in range(CHUNKS):
                for d in range(1, groups):
                    extra(j, d, s, True).start()

    def at(where, steps, among=None):
        who = s == where
        if among is not None:
            who = who & (owns if among else jnp.logical_not(owns))

        @pl.when(who)
        def _():
            for item, shard in steps:
                if shard < where:
                    from_below(item, shard)
                else:
                    from_above(item, shard)

    def all_of(kind, *shards):
        if kind == Q:
            return [
                (item, shard)
                for pair in zip(rising, pieces(Q))
                for item, shard in ((pair[shard[1]], shard[0]) for shard in shards)
            ]
        return [(item, shard) for item in pieces(kind) for shard in shards]

    if n == 4:
        below, above = 0, 1
        serve_writes(1)
        at(0, all_of(KV, 1))
        at(1, all_of(KV, 2, 0))
        at(2, all_of(KV, 3, 1))
        at(3, all_of(KV, 2))
        add_writes(1)
        at(0, all_of(Q, (1, above)))
        at(1, all_of(O, 2, 0), True)
        at(1, all_of(Q, (2, above), (0, below))[:6] + [((Q, 3), 2)])
        at(2, all_of(O, 3, 1), True)
        at(2, all_of(Q, (3, above), (1, below)))
        at(3, all_of(Q, (2, below)))
        ready_near()
        for t in range(3):
            project(t)
        serve_writes(2)
        at(0, all_of(KV, 2))
        at(1, all_of(KV, 3) + [((Q, 0), 0)])
        at(2, all_of(KV, 0))
        at(3, all_of(KV, 1))
        add_writes(2)
        at(0, all_of(Q, (2, above)) + all_of(KV, 3))
        at(1, all_of(O, 3)[:1], True)
        at(1, all_of(Q, (3, above)), False)
        at(2, all_of(O, 0)[:1], True)
        at(2, all_of(Q, (0, below)), False)
        at(3, all_of(Q, (1, below)))
        serve_writes(3)
        at(3, all_of(KV, 0))
        start_extras()
        add_writes(3)
    else:

        @pl.loop(1, n)
        def _(k):
            serve_writes(k)
            serve(KV, k)
            serve(O, k)
            serve(Q, k, True)
            add_writes(k)

        start_extras()
        ready_near()
        for t in range(CHUNKS):
            project(t)
        ready_far()
        for t in range(CHUNKS):
            project_far(t)

        @pl.when(inner)
        def _():
            for fall, rise in zip(pieces(Q), rising):
                from_below(rise, 0)
                from_above(fall, n - 1)

    @pl.when(jnp.logical_not(owns & inner))
    def _():
        own_copy(1).wait()

        if native:

            @pl.when(end)
            def _():
                dmixed[s] = lax.dot_general(
                    ups[g], all_o[lanes(s, span), :], NT, preferred_element_type=f32
                ).astype(bf16)

    memory[...] = state[...].astype(bf16)
    norm_rows(memory, 0)

    own_copy(0).wait()
    own_copy(2).wait()
    for item in pieces(KV):
        finish(item)
    for kind, to in ((0, keys), (1, values)):
        part = jnp.dot(
            normed[...], all_kv[:, kind * span : (kind + 1) * span], preferred_element_type=f32
        ).astype(bf16)
        for h in range(KV_HEADS):
            to[h] = part[:, h * HEAD : (h + 1) * HEAD]

    rowdots[...] = jnp.zeros_like(rowdots)

    if n == 4:
        at(1, all_of(O, 3)[1:], True)
        at(2, all_of(O, 0)[1:], True)
        project(3)
        at(1, all_of(Q, (3, above)), True)
        at(2, all_of(Q, (0, below))[:2], True)
        ready_far()
        project_far(0)
        at(2, all_of(Q, (0, below))[2:3], True)
        project_far(1)
        at(2, all_of(Q, (0, below))[3:], True)
        project_far(2)
        project_far(3)

    def attend(j):
        ready = owns & inner
        if native:
            ready = ready | (end & (j == s))

        @pl.when(jnp.logical_not(ready))
        def _():
            remote(
                dmixed_out.at[j, 0], dmixed.at[j], dsend.at[j, 0], drecv.at[j], beyond
            ).wait_recv()

        queries = jnp.dot(
            normed[MEM:, :], all_q[:, lanes(j, span)], preferred_element_type=f32
        ).astype(bf16)
        small = (queries.astype(f32) * HEAD ** (-0.5)).astype(bf16)
        key, value = keys[j], values[j]
        small_key = (key.astype(f32) * HEAD ** (-0.5)).astype(bf16)
        pulled = dmixed[j]
        dkey = jnp.zeros(key.shape, f32)
        dvalue = jnp.zeros(value.shape, f32)
        dquery = []
        for h in range(GROUP):
            at = slice(h * HEAD, (h + 1) * HEAD)
            query, dhead = small[:, at], pulled[:, at]
            scores = lax.dot_general(key, query, NT, preferred_element_type=f32) + bias[...]
            raised = jnp.exp(scores - jnp.max(scores, axis=0, keepdims=True))
            probs = raised * (1.0 / jnp.sum(raised, axis=0, keepdims=True))
            dprobs = lax.dot_general(value, dhead, NT, preferred_element_type=f32)
            drop = jnp.sum(probs * dprobs, axis=0, keepdims=True)
            dscores = (probs * (dprobs - drop)).astype(bf16)
            dvalue += jnp.dot(probs.astype(bf16), dhead, preferred_element_type=f32)
            dkey += jnp.dot(dscores, query, preferred_element_type=f32)
            dquery.append(lax.dot_general(small_key, dscores, TN, preferred_element_type=f32))
        dkey = dkey.astype(bf16)
        dvalue = dvalue.astype(bf16)
        dkeys[j] = dkey
        dvalues[j] = dvalue
        dquery = jnp.concatenate(dquery, axis=0).T.astype(bf16)
        dq[:, lanes(j, span)] = dquery
        rowdots[...] += jnp.sum(
            dkey.astype(f32) * key.astype(f32) + dvalue.astype(f32) * value.astype(f32),
            axis=-1,
            keepdims=True,
        )
        rowdots[MEM:, :] += jnp.sum(
            dquery.astype(f32) * queries.astype(f32), axis=-1, keepdims=True
        )

    def serve_end(t):
        j = turn(t)

        @pl.when(last)
        def _():
            from_below((Q, j), 0)

        @pl.when(first)
        def _():
            from_above((Q, j), n - 1)

    serve_end(0)
    serve_end(1)
    for t in range(CHUNKS):
        if t > 0 and t < CHUNKS - 1:
            serve_end(t + 1)
        j = turn(t)
        finish((Q, j))
        attend(j)

    dkv = jnp.concatenate(
        [dkeys[h] for h in range(KV_HEADS)] + [dvalues[h] for h in range(KV_HEADS)], axis=1
    )
    tile = 256
    scale = scales[...]
    coef = rowdots[...] * scale * scale * (1.0 / width)

    @pl.loop(0, width // tile)
    def _(t):
        at = lanes(t, tile)
        both = lax.dot_general(dkv, all_kv[at, :], NT, preferred_element_type=f32)
        ones = lax.dot_general(dq[...], all_q[at, :], NT, preferred_element_type=f32)
        strength = gain[:, at]
        grad_memory[:, at] = (
            both[:MEM] * strength * scale[:MEM] - memory[:, at].astype(f32) * coef[:MEM]
        ).astype(bf16)
        grad_rows[:, at] = (
            (both[MEM:] + ones) * strength * scale[MEM:]
            - rows_in[:, at].astype(f32) * coef[MEM:]
            + ups[g, :, at].astype(f32)
        ).astype(bf16)

    @pl.loop(0, n)
    def _(shard):
        @pl.when(shard < s)
        def _():
            for d in range(1, sections):
                write_peer(shard, d, c).wait_send()

        @pl.when((shard <= s) & (s < n - 1))
        def _():
            write_up(shard).wait_send()

    for kind in PIECES:
        for item in pieces(kind):
            drain(item)

    @pl.when(end)
    def _():
        pull_far().wait_send()
        for j in range(CHUNKS):
            for d in range(1, groups):
                extra(j, d, s, True).wait_send()

    @pl.when(inner & jnp.logical_not(owns))
    def _():
        pull_near().wait_send()

    @pl.when(inner & owns)
    def _():
        @pl.loop(0, CHUNKS)
        def _(j):
            @pl.loop(0, 2 * groups)
            def _(u):
                @pl.when((u < groups) & (u != g))
                def _():
                    give_back(j, u, s).wait_send()

                @pl.when((u >= groups) & near_end & sent_far(j))
                def _():
                    give_back(j, u, far).wait_send()


def per_device(
    n,
    groups,
    sections,
    writes,
    layer_inputs,
    upstream,
    pattern,
    w_q,
    w_kv,
    w_o,
    norm_gain,
    gate_weight,
    gate_bias,
):
    count, width = layer_inputs.shape[2:]
    total = MEM + count
    span = HEADS * HEAD // CHUNKS
    anywhere = pl.BlockSpec(memory_space=pl.ANY)
    near = pl.BlockSpec(memory_space=pltpu.VMEM)
    dma = pltpu.SemaphoreType.DMA
    bf16, f32 = jnp.bfloat16, jnp.float32
    grads = pl.pallas_call(
        functools.partial(layer_kernel, n, groups, sections),
        out_shape=[
            jax.ShapeDtypeStruct((count, width), bf16),
            jax.ShapeDtypeStruct((MEM, width), bf16),
        ],
        in_specs=[pl.BlockSpec(memory_space=pltpu.SMEM), anywhere, anywhere, anywhere]
        + [near] * 3
        + [anywhere] * 3,
        out_specs=[near, near],
        scratch_shapes=[
            pltpu.VMEM((count, width), bf16),
            pltpu.VMEM((2 * groups, count, width), bf16),
            pltpu.VMEM((n, MEM, width), bf16),
            pltpu.VMEM((width, w_kv.shape[2]), bf16),
            pltpu.VMEM((width, HEADS * HEAD), bf16),
            pltpu.VMEM((HEADS * HEAD, width), bf16),
            pltpu.VMEM((total, width), bf16),
            pltpu.VMEM((total, 1), f32),
            pltpu.VMEM((MEM, width), bf16),
            pltpu.VMEM((MEM, width), f32),
            pltpu.VMEM((MEM, HEADS), f32),
            pltpu.VMEM((3, HEADS, width), bf16),
            pltpu.VMEM((KV_HEADS, total, HEAD), bf16),
            pltpu.VMEM((KV_HEADS, total, HEAD), bf16),
            pltpu.VMEM((total, count), f32),
            pltpu.VMEM((KV_HEADS, count, span), bf16),
            pltpu.VMEM((KV_HEADS, 2 * groups, count, span), bf16),
            pltpu.VMEM((count, HEADS * HEAD), bf16),
            pltpu.VMEM((KV_HEADS, total, HEAD), bf16),
            pltpu.VMEM((KV_HEADS, total, HEAD), bf16),
            pltpu.VMEM((total, 1), f32),
            dma((ITEMS, n)),
            dma((ITEMS, n)),
            dma((ITEMS, n)),
            dma((CHUNKS, groups)),
            dma((CHUNKS, groups)),
            dma((O, n, groups)),
            dma((O, n, groups)),
            dma((n,)),
            dma((n,)),
            dma((n, sections)),
            dma((n, sections)),
            dma((1,)),
            dma((2 * groups,)),
            dma((CHUNKS, 2 * groups)),
            dma((CHUNKS,)),
            dma((5,)),
        ],
        compiler_params=pltpu.CompilerParams(
            collective_id=0, has_side_effects=True, vmem_limit_bytes=56 * 1024 * 1024
        ),
    )(
        pattern[0],
        writes[0],
        layer_inputs[0, 0],
        upstream[0, 0],
        norm_gain,
        gate_weight[0].T,
        gate_bias,
        w_kv[0],
        w_q[0],
        w_o[0],
    )
    return (grads[0][None, None], grads[1][None, None])


def solution(mesh):
    placed = (
        P(("groups", "seg"), None, "section"),
        P("section", ("groups", "seg"), None, None),
        P("section", ("groups", "seg"), None, None),
        P(("groups", "seg"), None, None),
        P("section", "seg", None),
        P("section", "seg", None),
        P("section", "seg", None),
        P("section", None),
        P("section", None, None),
        P("section", None),
    )
    sizes = (mesh.shape["seg"], mesh.shape["groups"], mesh.shape["section"])
    return jax.shard_map(
        functools.partial(per_device, *sizes),
        mesh=mesh,
        in_specs=placed,
        out_specs=(
            P("section", ("groups", "seg"), None, None),
            P("section", ("groups", "seg"), None, None),
        ),
        check_vma=False,
    )
```

```python
import functools

import jax
import jax.numpy as jnp
from jax import lax
from jax.experimental import pallas as pl
from jax.experimental.pallas import tpu as pltpu
from jax.sharding import PartitionSpec as P

HEADS = 16
KV_HEADS = 4
HEAD = 64
BLK = 128
MEM = 128


epsilon = 1e-05
masked_score = -1e30
GROUP = HEADS // KV_HEADS
NT = (((1,), (1,)), ((), ()))
TN = (((0,), (0,)), ((), ()))
CHUNKS = KV_HEADS
PAIR = 2
STRIPS = 4
KV, Q, O = 0, PAIR, PAIR + CHUNKS
PIECES = {KV: PAIR, Q: CHUNKS, O: STRIPS}
ITEMS = PAIR + CHUNKS + STRIPS
MESH = pl.DeviceIdType.MESH


def layer_kernel(
    n,
    groups,
    sections,
    pattern,
    writes,
    rows_far,
    up_far,
    gain,
    gate,
    gate_bias,
    w_kv,
    w_q,
    w_o,
    out_rows,
    out_memory,
    grad_rows,
    grad_memory,
    rows_in,
    ups,
    all_writes,
    all_kv,
    all_q,
    all_o,
    normed,
    scales,
    memory,
    state,
    passed,
    gates,
    keys,
    values,
    bias,
    dmixed,
    dmixed_out,
    dq,
    dkeys,
    dvalues,
    rowdots,
    *sems,
):
    (
        up_sem,
        down_sem,
        zrecv,
        xsend,
        xrecv,
        ysend,
        yrecv,
        wsend,
        wrecv,
        psend,
        precv,
        usend,
        urecv,
        dsend,
        drecv,
        local,
        leave,
    ) = sems
    g = lax.axis_index("groups")
    s = lax.axis_index("seg")
    c = lax.axis_index("section")
    count, width = rows_in.shape
    wide = writes.shape[1]
    span = all_q.shape[1] // CHUNKS
    half_kv = all_kv.shape[1] // PAIR
    f32, bf16 = jnp.float32, jnp.bfloat16
    native = n == CHUNKS

    owner = lax.rem(c, groups)
    owns = g == owner
    first, last = s == 0, s == n - 1
    end = first | last
    inner = jnp.logical_not(end)
    near_end = (s == 1) | (s == n - 2)
    far = jnp.where(s == 1, 0, n - 1)
    inward = jnp.where(first, 1, n - 2)

    def lanes(at, size):
        return pl.ds(pl.multiple_of(at * size, size), size)

    mine = lanes(c, wide)

    barrier = pltpu.get_barrier_semaphore()

    def greet(where):
        pl.semaphore_signal(barrier, inc=1, device_id=where, device_id_type=MESH)

    @pl.when(s > 0)
    def _():
        greet((g, s - 1, c))

    @pl.when(s < n - 1)
    def _():
        greet((g, s + 1, c))

    for d in range(1, groups):
        greet((lax.rem(g + d, groups), s, c))

        @pl.when(end)
        def _():
            greet((lax.rem(g + d, groups), inward, c))

        @pl.when(near_end)
        def _():
            greet((lax.rem(g + d, groups), far, c))

    for d in range(1, sections):
        greet((g, s, lax.rem(c + d, sections)))

    def input_copy(k):
        if k == 0:
            return pltpu.make_async_copy(rows_far, rows_in, local.at[3])
        return pltpu.make_async_copy(up_far, ups.at[g], local.at[4])

    input_copy(0).start()
    input_copy(1).start()

    beside = jnp.where(end, 1, 2) + jnp.where(end | near_end, groups - 1, 0)
    pl.semaphore_wait(barrier, beside + groups + sections - 2)

    def remote(src, dst, send, recv, where):
        return pltpu.make_async_remote_copy(
            src_ref=src,
            dst_ref=dst,
            send_sem=send,
            recv_sem=recv,
            device_id=where,
            device_id_type=MESH,
        )

    def operand(kind):
        return {
            KV: (w_kv, all_kv, half_kv),
            Q: (w_q, all_q, span),
            O: (w_o, all_o, width // STRIPS),
        }[kind]

    def columns(kind, chunk):
        cols = operand(kind)[2]
        if isinstance(chunk, int):
            return slice(chunk * cols, (chunk + 1) * cols)
        return lanes(chunk, cols)

    def spot(item, shard, part):
        kind, chunk = item
        src, dst, _ = operand(kind)
        at = columns(kind, chunk)
        if kind == O:
            return dst.at[lanes(shard, src.shape[0]), at]
        half = src.shape[0] // groups
        return dst.at[lanes(shard * groups + part, half), at]

    def source(item, part):
        kind, chunk = item
        src = operand(kind)[0]
        at = columns(kind, chunk)
        if kind == O:
            return src.at[:, at]
        return src.at[lanes(part, src.shape[0] // groups), at]

    def up(item, shard, own=False):
        i, there = item[0] + item[1], spot(item, shard, g)
        src = source(item, g) if own else there
        return remote(src, there, up_sem.at[i, shard], zrecv.at[i, shard], (g, s + 1, c))

    def down(item, shard, own=False):
        i, there = item[0] + item[1], spot(item, shard, g)
        src = source(item, g) if own else there
        return remote(src, there, down_sem.at[i, shard], zrecv.at[i, shard], (g, s - 1, c))

    def extra(j, d, shard, own=False):
        part = lax.rem(g + d, groups)
        there = spot((Q, j), shard, part)
        src = source((Q, j), part) if own else there
        return remote(src, there, xsend.at[j, d], xrecv.at[j, d], (g, inward, c))

    def across(item, shard, d, part):
        i, there = item[0] + item[1], spot(item, shard, part)
        return remote(
            there,
            there,
            ysend.at[i, shard, d],
            yrecv.at[i, shard, d],
            (lax.rem(g + d, groups), s, c),
        )

    def write_up(shard, own=False):
        there = all_writes.at[shard, :, mine]
        return remote(
            writes if own else there, there, wsend.at[shard], wrecv.at[shard], (g, s + 1, c)
        )

    def write_peer(shard, d, origin):
        there = all_writes.at[shard, :, lanes(origin, wide)]
        return remote(
            there,
            there,
            psend.at[shard, d],
            precv.at[shard, d],
            (g, s, lax.rem(c + d, sections)),
        )

    def pull_near():
        return remote(up_far, ups.at[g], usend.at[0], urecv.at[g], (owner, s, c))

    def pull_far():
        at = groups + g
        return remote(up_far, ups.at[at], usend.at[0], urecv.at[at], (owner, inward, c))

    def give_back(j, u, where):
        return remote(
            dmixed_out.at[j, u],
            dmixed.at[j],
            dsend.at[j, u],
            drecv.at[j],
            (lax.rem(u, groups), where, c),
        )

    def own_copy(w):
        src, dst = ((w_kv, all_kv), (w_o, all_o), (w_q, all_q))[w]
        return pltpu.make_async_copy(src, dst.at[lanes(s, src.shape[0]), :], local.at[w])

    def rises(kind):
        return (owns & (s > 0) & (s < n - 2)) | (owns & first) if kind == O else s < n - 1

    def falls(kind):
        return (owns & (s < n - 1) & (s > 1)) | (owns & last) if kind == O else s > 0

    def skips(kind, shard):
        if kind != Q:
            return shard < 0
        return ((shard == 0) & (s == 1)) | ((shard == n - 1) & (s == n - 2))

    def pieces(kind):
        return [(kind, k) for k in range(PIECES[kind])]

    rising = list(reversed(pieces(Q)))

    def start_own(kind):
        for fall in pieces(kind):
            rise = (kind, CHUNKS - 1 - fall[1]) if kind == Q else fall

            @pl.when(rises(kind))
            def _():
                up(rise, s, True).start()

            @pl.when(falls(kind))
            def _():
                down(fall, s, True).start()

    def spread(item, shard):
        if item[0] == O:
            return

        def send():
            for d in range(1, groups):
                across(item, shard, d, g).start()

        if item[0] == KV:
            send()
        else:
            pl.when(jnp.logical_not(skips(Q, shard)))(send)

    def from_below(item, shard):
        up(item, shard).wait_recv()

        @pl.when(rises(item[0]))
        def _():
            up(item, shard).start()

        spread(item, shard)

    def from_above(item, shard):
        down(item, shard).wait_recv()

        @pl.when(falls(item[0]))
        def _():
            down(item, shard).start()

        spread(item, shard)

    def reaches(kind):
        return owns & inner if kind == O else s >= 0

    def serve(kind, k, inside=False):
        low = 1 if inside else 0

        @pl.when((s - k >= low) & reaches(kind))
        def _():
            for item in rising if kind == Q else pieces(kind):
                from_below(item, s - k)

        @pl.when((s + k < n - low) & reaches(kind))
        def _():
            for item in pieces(kind):
                from_above(item, s + k)

    def finish(item):
        @pl.loop(0, n)
        def _(shard):
            skipped = skips(item[0], shard)

            @pl.when((shard != s) & jnp.logical_not(skipped))
            def _():
                for d in range(1, groups):
                    across(item, shard, d, lax.rem(g + groups - d, groups)).wait_recv()

            if item[0] == Q:

                @pl.when(skipped)
                def _():
                    for d in range(1, groups):
                        extra(item[1], d, shard).wait_recv()

    def drain(item):
        kind = item[0]

        @pl.loop(0, n)
        def _(shard):
            if kind != O:

                @pl.when((shard != s) & jnp.logical_not(skips(kind, shard)))
                def _():
                    for d in range(1, groups):
                        across(item, shard, d, g).wait_send()

            @pl.when((shard <= s) & rises(kind))
            def _():
                up(item, shard).wait_send()

            @pl.when((shard >= s) & falls(kind))
            def _():
                down(item, shard).wait_send()

    @pl.when(s < n - 1)
    def _():
        write_up(s, True).start()

    start_own(KV)

    @pl.when(inner & jnp.logical_not(owns))
    def _():
        pull_near().start()

    @pl.when(end & jnp.logical_not(owns))
    def _():
        pull_far().start()

    pl.when(first)(lambda: start_own(Q))
    start_own(O)
    pl.when(s > 0)(lambda: start_own(Q))

    @pl.when(end & owns)
    def _():
        pull_far().start()

    @pl.when(end)
    def _():
        for j in range(CHUNKS):
            for d in range(1, groups):
                extra(j, d, s, True).start()

    for w in range(3):
        own_copy(w).start()

    strip = 32

    def norm_rows(from_ref, to_row):
        @pl.loop(0, from_ref.shape[0] // strip)
        def _(r):
            x = from_ref[lanes(r, strip), :].astype(f32)
            scale = lax.rsqrt(jnp.mean(x * x, axis=-1, keepdims=True) + epsilon)
            to = pl.ds(pl.multiple_of(to_row + r * strip, strip), strip)
            normed[to, :] = (x * scale * gain[...]).astype(bf16)
            scales[to, :] = scale

    input_copy(0).wait()
    input_copy(1).wait()
    norm_rows(rows_in, MEM)

    whole_gate = gate[...]
    high = whole_gate.astype(bf16)
    rest = whole_gate - high.astype(f32)
    middle = rest.astype(bf16)
    gates[0] = high
    gates[1] = middle
    gates[2] = (rest - middle.astype(f32)).astype(bf16)

    keyed = lax.broadcasted_iota(jnp.int32, (BLK, BLK), 0)
    asked = lax.broadcasted_iota(jnp.int32, (BLK, BLK), 1)
    blocks = count // BLK
    for b in range(blocks):
        seen = jnp.where(pattern[b, 0] > 0, 0.0, masked_score)
        parts = [jnp.full((MEM, BLK), seen, f32)]
        for e in range(b):
            seen = jnp.where(pattern[b, 1 + e] > 0, 0.0, masked_score)
            parts.append(jnp.full((BLK, BLK), seen, f32))
        parts.append(jnp.where(keyed <= asked, 0.0, masked_score).astype(f32))
        for e, part in enumerate(parts):
            for r in range(PAIR):
                bias[b, e * BLK : (e + 1) * BLK, r * BLK : (r + 1) * BLK] = part

    state[...] = jnp.zeros_like(state)
    passed[...] = jnp.ones_like(passed)
    cut = width // HEADS

    def serve_writes(k):
        @pl.when(s - k >= 0)
        def _():
            write_up(s - k).wait_recv()

            @pl.when(s < n - 1)
            def _():
                write_up(s - k).start()

            for d in range(1, sections):
                write_peer(s - k, d, c).start()

    def add_writes(k):
        @pl.when(s - k >= 0)
        def _():
            for d in range(1, sections):
                write_peer(s - k, d, lax.rem(c + sections - d, sections)).wait_recv()
            w = all_writes[s - k]
            logits = sum(
                lax.dot_general(w, gates[p], NT, preferred_element_type=f32) for p in range(3)
            )
            keep = jax.nn.sigmoid(logits + gate_bias[...])
            fresh = passed[...] * (1.0 - keep)
            passed[...] = passed[...] * keep
            for h in range(HEADS):
                at = slice(h * cut, (h + 1) * cut)
                state[:, at] += fresh[:, h : h + 1] * w[:, at].astype(f32)

    def turn(t):
        return jnp.where(s < n // 2, t, CHUNKS - 1 - t)

    def sent_far(j):
        return (j != far) if native else (j >= 0)

    def give_all(t, away):
        j = turn(t)
        base = groups if away else 0
        weight = all_o[lanes(j, span), :]
        pulled = ups[base : base + groups].reshape(groups * count, width)
        part = lax.dot_general(pulled, weight, NT, preferred_element_type=f32).astype(bf16)
        for u in range(groups):
            piece = part[u * count : (u + 1) * count]
            dmixed_out[j, base + u] = piece
            if away:

                @pl.when(sent_far(j))
                def _():
                    give_back(j, base + u, far).start()

            else:

                @pl.when(u == g)
                def _():
                    dmixed[j] = piece

                @pl.when(u != g)
                def _():
                    give_back(j, u, s).start()

    def project(t):
        pl.when(owns & inner)(lambda: give_all(t, False))

    def project_far(t):
        pl.when(owns & near_end)(lambda: give_all(t, True))

    beyond = (lax.rem(g + 1, groups), s, c)

    def wait_pulls(low, high):
        @pl.loop(low, high)
        def _(u):
            @pl.when(u != g)
            def _():
                remote(up_far, ups.at[u], usend.at[0], urecv.at[u], beyond).wait_recv()

    def ready_near():
        @pl.when(owns & inner)
        def _():
            own_copy(1).wait()
            wait_pulls(0, groups)

    def ready_far():
        @pl.when(owns & near_end)
        def _():
            wait_pulls(groups, 2 * groups)

    def at(where, steps, among=None):
        who = s == where
        if among is not None:
            who = who & (owns if among else jnp.logical_not(owns))

        @pl.when(who)
        def _():
            for item, shard in steps:
                if shard < where:
                    from_below(item, shard)
                else:
                    from_above(item, shard)

    def all_of(items, *shards):
        return [(item, shard) for item in items for shard in shards]

    if n == 4:
        kvs, qs, os = pieces(KV), pieces(Q), pieces(O)
        serve_writes(1)
        at(0, all_of(kvs, 1))
        at(1, all_of(kvs, 2, 0))
        at(2, all_of(kvs, 3, 1))
        at(3, all_of(kvs, 2))
        add_writes(1)
        at(0, all_of(qs, 1))
        ups_0, downs_2, o_0, o_2 = (
            all_of(rising, 0),
            all_of(qs, 2),
            all_of(os, 0),
            all_of(os, 2),
        )
        at(
            1,
            o_2[:1]
            + ups_0[:2]
            + o_2[1:2]
            + ups_0[2:]
            + o_2[2:3]
            + o_0[:1]
            + o_2[3:]
            + downs_2[:3]
            + o_0[1:2]
            + downs_2[3:],
            True,
        )
        at(1, downs_2, False)
        ups_1, downs_3 = all_of(rising, 1), all_of(qs, 3)
        at(
            2,
            all_of(os, 3, 1)
            + downs_3[:1]
            + ups_1[:3]
            + downs_3[1:2]
            + ups_1[3:]
            + downs_3[2:3],
            True,
        )
        at(2, ups_1, False)
        at(3, all_of(rising, 2))
        serve_writes(2)
        at(0, all_of(kvs, 2))
        at(1, all_of(kvs, 3))
        at(1, o_0[2:3], True)
        at(2, downs_3[3:], True)
        at(2, all_of(kvs, 0))
        at(3, all_of(kvs, 1))
        add_writes(2)
        at(0, all_of(qs, 2) + all_of(kvs, 3))
        at(1, all_of(os, 3)[:1] + o_0[3:], True)
        mixed_steps = [step for pair in zip(ups_0, downs_3) for step in pair]
        at(1, mixed_steps, False)
        at(2, ups_0, True)
        at(2, downs_3[:3] + ups_0[:1] + downs_3[3:] + ups_0[1:], False)
        at(3, all_of(rising, 1))
        serve_writes(3)
        at(3, all_of(kvs, 0))
        ready_near()
        for t in range(3):
            project(t)
        add_writes(3)
    else:

        @pl.loop(1, n)
        def _(k):
            serve_writes(k)
            serve(KV, k)
            serve(O, k)
            serve(Q, k, True)
            add_writes(k)

        ready_near()
        for t in range(CHUNKS):
            project(t)
        ready_far()
        for t in range(CHUNKS):
            project_far(t)

        @pl.when(inner)
        def _():
            for fall, rise in zip(pieces(Q), rising):
                from_below(rise, 0)
                from_above(fall, n - 1)

    @pl.when(jnp.logical_not(owns & inner))
    def _():
        own_copy(1).wait()

        if native:

            @pl.when(end)
            def _():
                dmixed[s] = lax.dot_general(
                    ups[g], all_o[lanes(s, span), :], NT, preferred_element_type=f32
                ).astype(bf16)

    if n == 4:
        at(1, all_of(os, 3)[1:] + downs_3, True)

    memory[...] = state[...].astype(bf16)
    norm_rows(memory, 0)

    own_copy(0).wait()
    own_copy(2).wait()
    for item in pieces(KV):
        finish(item)
    for kind, to in ((0, keys), (1, values)):
        part = jnp.dot(
            normed[...], all_kv[:, kind * span : (kind + 1) * span], preferred_element_type=f32
        ).astype(bf16)
        for h in range(KV_HEADS):
            to[h] = part[:, h * HEAD : (h + 1) * HEAD]

    rowdots[...] = jnp.zeros_like(rowdots)

    if n == 4:
        at(2, o_0[:2], True)
        ready_far()
        project_far(1)
        project_far(2)
        at(2, o_0[2:], True)
        project(3)
        project_far(3)

    def attend(j):
        ready = owns & inner
        if native:
            ready = ready | (end & (j == s))

        @pl.when(jnp.logical_not(ready))
        def _():
            remote(
                dmixed_out.at[j, 0], dmixed.at[j], dsend.at[j, 0], drecv.at[j], beyond
            ).wait_recv()

        queries = jnp.dot(
            normed[MEM:, :], all_q[:, lanes(j, span)], preferred_element_type=f32
        ).astype(bf16)
        small = (queries.astype(f32) * HEAD ** (-0.5)).astype(bf16)
        key, value = keys[j], values[j]
        small_key = (key.astype(f32) * HEAD ** (-0.5)).astype(bf16)
        pulled = dmixed[j]
        dkey = [jnp.zeros((BLK, HEAD), f32) for _ in range(blocks + 1)]
        dvalue = [jnp.zeros((BLK, HEAD), f32) for _ in range(blocks + 1)]
        dquery = [[None] * blocks for _ in range(GROUP)]
        for h in range(0, GROUP, PAIR):
            for b in range(blocks):
                rows = slice(b * BLK, (b + 1) * BLK)
                depth = MEM + (b + 1) * BLK

                def stacked(x):
                    return jnp.concatenate(
                        [x[rows, (h + r) * HEAD : (h + r + 1) * HEAD] for r in range(PAIR)], axis=0
                    )

                query, dhead = stacked(small), stacked(pulled)
                scores = lax.dot_general(key[:depth], query, NT, preferred_element_type=f32)
                scores = scores + bias[b, :depth, :]
                raised = jnp.exp(scores - jnp.max(scores, axis=0, keepdims=True))
                probs = raised * (1.0 / jnp.sum(raised, axis=0, keepdims=True))
                dprobs = lax.dot_general(value[:depth], dhead, NT, preferred_element_type=f32)
                drop = jnp.sum(probs * dprobs, axis=0, keepdims=True)
                dscores = (probs * (dprobs - drop)).astype(bf16)
                dv = jnp.dot(probs.astype(bf16), dhead, preferred_element_type=f32)
                dk = jnp.dot(dscores, query, preferred_element_type=f32)
                for e in range(depth // BLK):
                    dvalue[e] += dv[e * BLK : (e + 1) * BLK]
                    dkey[e] += dk[e * BLK : (e + 1) * BLK]
                back = lax.dot_general(small_key[:depth], dscores, TN, preferred_element_type=f32)
                for r in range(PAIR):
                    dquery[h + r][b] = back[:, r * BLK : (r + 1) * BLK]
        dquery = [jnp.concatenate(parts, axis=1) for parts in dquery]
        dkey = jnp.concatenate(dkey, axis=0)
        dvalue = jnp.concatenate(dvalue, axis=0)
        dkey = dkey.astype(bf16)
        dvalue = dvalue.astype(bf16)
        dkeys[j] = dkey
        dvalues[j] = dvalue
        dquery = jnp.concatenate(dquery, axis=0).T.astype(bf16)
        dq[:, lanes(j, span)] = dquery
        rowdots[...] += jnp.sum(
            dkey.astype(f32) * key.astype(f32) + dvalue.astype(f32) * value.astype(f32),
            axis=-1,
            keepdims=True,
        )
        rowdots[MEM:, :] += jnp.sum(
            dquery.astype(f32) * queries.astype(f32), axis=-1, keepdims=True
        )

    def serve_end(t):
        j = turn(t)

        @pl.when(last)
        def _():
            from_below((Q, j), 0)

        @pl.when(first)
        def _():
            from_above((Q, j), n - 1)

    serve_end(0)
    serve_end(1)
    for t in range(CHUNKS):
        if t > 0 and t < CHUNKS - 1:
            serve_end(t + 1)
        j = turn(t)
        finish((Q, j))
        attend(j)

    dkv = jnp.concatenate(
        [dkeys[h] for h in range(KV_HEADS)] + [dvalues[h] for h in range(KV_HEADS)], axis=1
    )
    tile = 256
    scale = scales[...]
    coef = rowdots[...] * scale * scale * (1.0 / width)

    def leaving(t):
        at = lanes(t, tile)
        return (
            pltpu.make_async_copy(grad_rows.at[:, at], out_rows.at[:, at], leave.at[0, t]),
            pltpu.make_async_copy(grad_memory.at[:, at], out_memory.at[:, at], leave.at[1, t]),
        )

    @pl.loop(0, width // tile, unroll=8)
    def _(t):
        at = lanes(t, tile)
        both = lax.dot_general(dkv, all_kv[at, :], NT, preferred_element_type=f32)
        ones = lax.dot_general(dq[...], all_q[at, :], NT, preferred_element_type=f32)
        strength = gain[:, at]
        grad_memory[:, at] = (
            both[:MEM] * strength * scale[:MEM] - memory[:, at].astype(f32) * coef[:MEM]
        ).astype(bf16)
        grad_rows[:, at] = (
            (both[MEM:] + ones) * strength * scale[MEM:]
            - rows_in[:, at].astype(f32) * coef[MEM:]
            + ups[g, :, at].astype(f32)
        ).astype(bf16)
        for copy in leaving(t):
            copy.start()

    @pl.loop(0, n)
    def _(shard):
        @pl.when(shard < s)
        def _():
            for d in range(1, sections):
                write_peer(shard, d, c).wait_send()

        @pl.when((shard <= s) & (s < n - 1))
        def _():
            write_up(shard).wait_send()

    for kind in PIECES:
        for item in pieces(kind):
            drain(item)

    @pl.when(end)
    def _():
        pull_far().wait_send()
        for j in range(CHUNKS):
            for d in range(1, groups):
                extra(j, d, s, True).wait_send()

    @pl.when(inner & jnp.logical_not(owns))
    def _():
        pull_near().wait_send()

    @pl.loop(0, width // tile)
    def _(t):
        for copy in leaving(t):
            copy.wait()

    @pl.when(inner & owns)
    def _():
        @pl.loop(0, CHUNKS)
        def _(j):
            @pl.loop(0, 2 * groups)
            def _(u):
                @pl.when((u < groups) & (u != g))
                def _():
                    give_back(j, u, s).wait_send()

                @pl.when((u >= groups) & near_end & sent_far(j))
                def _():
                    give_back(j, u, far).wait_send()


def hand_over(rows_from, memory_from, rows_to, memory_to, sems):
    cut = memory_from.shape[0] // 2
    copies = [
        pltpu.make_async_copy(
            src.at[k * cut : (k + 1) * cut, :], dst.at[k * cut : (k + 1) * cut, :], sems.at[w, k]
        )
        for w, (src, dst) in enumerate(((rows_from, rows_to), (memory_from, memory_to)))
        for k in range(src.shape[0] // cut)
    ]
    for copy in copies:
        copy.start()
    for copy in copies:
        copy.wait()


def per_device(
    n,
    groups,
    sections,
    writes,
    layer_inputs,
    upstream,
    pattern,
    w_q,
    w_kv,
    w_o,
    norm_gain,
    gate_weight,
    gate_bias,
):
    count, width = layer_inputs.shape[2:]
    total = MEM + count
    span = HEADS * HEAD // CHUNKS
    anywhere = pl.BlockSpec(memory_space=pl.ANY)
    near = pl.BlockSpec(memory_space=pltpu.VMEM)
    dma = pltpu.SemaphoreType.DMA
    bf16, f32 = jnp.bfloat16, jnp.float32
    grads = pl.pallas_call(
        functools.partial(layer_kernel, n, groups, sections),
        out_shape=[
            jax.ShapeDtypeStruct((count, width), bf16),
            jax.ShapeDtypeStruct((MEM, width), bf16),
        ],
        in_specs=[pl.BlockSpec(memory_space=pltpu.SMEM), anywhere, anywhere, anywhere]
        + [near] * 3
        + [anywhere] * 3,
        out_specs=[anywhere, anywhere],
        scratch_shapes=[
            pltpu.VMEM((count, width), bf16),
            pltpu.VMEM((MEM, width), bf16),
            pltpu.VMEM((count, width), bf16),
            pltpu.VMEM((2 * groups, count, width), bf16),
            pltpu.VMEM((n, MEM, width), bf16),
            pltpu.VMEM((width, w_kv.shape[2]), bf16),
            pltpu.VMEM((width, HEADS * HEAD), bf16),
            pltpu.VMEM((HEADS * HEAD, width), bf16),
            pltpu.VMEM((total, width), bf16),
            pltpu.VMEM((total, 1), f32),
            pltpu.VMEM((MEM, width), bf16),
            pltpu.VMEM((MEM, width), f32),
            pltpu.VMEM((MEM, HEADS), f32),
            pltpu.VMEM((3, HEADS, width), bf16),
            pltpu.VMEM((KV_HEADS, total, HEAD), bf16),
            pltpu.VMEM((KV_HEADS, total, HEAD), bf16),
            pltpu.VMEM((count // BLK, total, PAIR * BLK), f32),
            pltpu.VMEM((KV_HEADS, count, span), bf16),
            pltpu.VMEM((KV_HEADS, 2 * groups, count, span), bf16),
            pltpu.VMEM((count, HEADS * HEAD), bf16),
            pltpu.VMEM((KV_HEADS, total, HEAD), bf16),
            pltpu.VMEM((KV_HEADS, total, HEAD), bf16),
            pltpu.VMEM((total, 1), f32),
            dma((ITEMS, n)),
            dma((ITEMS, n)),
            dma((ITEMS, n)),
            dma((CHUNKS, groups)),
            dma((CHUNKS, groups)),
            dma((O, n, groups)),
            dma((O, n, groups)),
            dma((n,)),
            dma((n,)),
            dma((n, sections)),
            dma((n, sections)),
            dma((1,)),
            dma((2 * groups,)),
            dma((CHUNKS, 2 * groups)),
            dma((CHUNKS,)),
            dma((5,)),
            dma((2, width // 256)),
        ],
        compiler_params=pltpu.CompilerParams(
            collective_id=0, has_side_effects=True, vmem_limit_bytes=56 * 1024 * 1024
        ),
    )(
        pattern[0],
        writes[0],
        layer_inputs[0, 0],
        upstream[0, 0],
        norm_gain,
        gate_weight[0].T,
        gate_bias,
        w_kv[0],
        w_q[0],
        w_o[0],
    )
    return (grads[0][None, None], grads[1][None, None])


def solution(mesh):
    placed = (
        P(("groups", "seg"), None, "section"),
        P("section", ("groups", "seg"), None, None),
        P("section", ("groups", "seg"), None, None),
        P(("groups", "seg"), None, None),
        P("section", "seg", None),
        P("section", "seg", None),
        P("section", "seg", None),
        P("section", None),
        P("section", None, None),
        P("section", None),
    )
    sizes = (mesh.shape["seg"], mesh.shape["groups"], mesh.shape["section"])
    return jax.shard_map(
        functools.partial(per_device, *sizes),
        mesh=mesh,
        in_specs=placed,
        out_specs=(
            P("section", ("groups", "seg"), None, None),
            P("section", ("groups", "seg"), None, None),
        ),
        check_vma=False,
    )
```

```python
import functools

import jax
import jax.numpy as jnp
from jax import lax
from jax.experimental import pallas as pl
from jax.experimental.pallas import tpu as pltpu
from jax.sharding import PartitionSpec as P

HEADS = 16
KV_HEADS = 4
HEAD = 64
BLK = 128
MEM = 128


epsilon = 1e-05
masked_score = -1e30
GROUP = HEADS // KV_HEADS
NT = (((1,), (1,)), ((), ()))
TN = (((0,), (0,)), ((), ()))
CHUNKS = KV_HEADS
PAIR = 2
STRIPS = 4
KV, Q, O = 0, PAIR, PAIR + CHUNKS
PIECES = {KV: PAIR, Q: CHUNKS, O: STRIPS}
ITEMS = PAIR + CHUNKS + STRIPS
MESH = pl.DeviceIdType.MESH


def layer_kernel(
    n,
    groups,
    sections,
    pattern,
    writes,
    rows_far,
    up_far,
    gain,
    gate,
    gate_bias,
    w_kv,
    w_q,
    w_o,
    out_rows,
    out_memory,
    grad_rows,
    grad_memory,
    rows_in,
    ups,
    all_writes,
    all_kv,
    all_q,
    all_o,
    normed,
    scales,
    memory,
    state,
    passed,
    gates,
    keys,
    values,
    bias,
    dmixed,
    dmixed_out,
    dq,
    dkeys,
    dvalues,
    rowdots,
    *sems,
):
    (
        up_sem,
        down_sem,
        zrecv,
        xsend,
        xrecv,
        ysend,
        yrecv,
        wsend,
        wrecv,
        psend,
        precv,
        usend,
        urecv,
        dsend,
        drecv,
        local,
        leave,
    ) = sems
    g = lax.axis_index("groups")
    s = lax.axis_index("seg")
    c = lax.axis_index("section")
    count, width = rows_in.shape
    wide = writes.shape[1]
    span = all_q.shape[1] // CHUNKS
    half_kv = all_kv.shape[1] // PAIR
    f32, bf16 = jnp.float32, jnp.bfloat16
    native = n == CHUNKS

    owner = lax.rem(c, groups)
    owns = g == owner
    first, last = s == 0, s == n - 1
    end = first | last
    inner = jnp.logical_not(end)
    near_end = (s == 1) | (s == n - 2)
    far = jnp.where(s == 1, 0, n - 1)
    inward = jnp.where(first, 1, n - 2)

    def lanes(at, size):
        return pl.ds(pl.multiple_of(at * size, size), size)

    mine = lanes(c, wide)

    barrier = pltpu.get_barrier_semaphore()

    def greet(where):
        pl.semaphore_signal(barrier, inc=1, device_id=where, device_id_type=MESH)

    @pl.when(s > 0)
    def _():
        greet((g, s - 1, c))

    @pl.when(s < n - 1)
    def _():
        greet((g, s + 1, c))

    for d in range(1, groups):
        greet((lax.rem(g + d, groups), s, c))

        @pl.when(end)
        def _():
            greet((lax.rem(g + d, groups), inward, c))

        @pl.when(near_end)
        def _():
            greet((lax.rem(g + d, groups), far, c))

    for d in range(1, sections):
        greet((g, s, lax.rem(c + d, sections)))

    def input_copy(k):
        if k == 0:
            return pltpu.make_async_copy(rows_far, rows_in, local.at[3])
        return pltpu.make_async_copy(up_far, ups.at[g], local.at[4])

    input_copy(0).start()
    input_copy(1).start()

    beside = jnp.where(end, 1, 2) + jnp.where(end | near_end, groups - 1, 0)
    pl.semaphore_wait(barrier, beside + groups + sections - 2)

    def remote(src, dst, send, recv, where):
        return pltpu.make_async_remote_copy(
            src_ref=src,
            dst_ref=dst,
            send_sem=send,
            recv_sem=recv,
            device_id=where,
            device_id_type=MESH,
        )

    def operand(kind):
        return {
            KV: (w_kv, all_kv, half_kv),
            Q: (w_q, all_q, span),
            O: (w_o, all_o, width // STRIPS),
        }[kind]

    def columns(kind, chunk):
        cols = operand(kind)[2]
        if isinstance(chunk, int):
            return slice(chunk * cols, (chunk + 1) * cols)
        return lanes(chunk, cols)

    def spot(item, shard, part):
        kind, chunk = item
        src, dst, _ = operand(kind)
        at = columns(kind, chunk)
        if kind == O:
            return dst.at[lanes(shard, src.shape[0]), at]
        half = src.shape[0] // groups
        return dst.at[lanes(shard * groups + part, half), at]

    def source(item, part):
        kind, chunk = item
        src = operand(kind)[0]
        at = columns(kind, chunk)
        if kind == O:
            return src.at[:, at]
        return src.at[lanes(part, src.shape[0] // groups), at]

    def up(item, shard, own=False):
        i, there = item[0] + item[1], spot(item, shard, g)
        src = source(item, g) if own else there
        return remote(src, there, up_sem.at[i, shard], zrecv.at[i, shard], (g, s + 1, c))

    def down(item, shard, own=False):
        i, there = item[0] + item[1], spot(item, shard, g)
        src = source(item, g) if own else there
        return remote(src, there, down_sem.at[i, shard], zrecv.at[i, shard], (g, s - 1, c))

    def extra(j, d, shard, own=False):
        part = lax.rem(g + d, groups)
        there = spot((Q, j), shard, part)
        src = source((Q, j), part) if own else there
        return remote(src, there, xsend.at[j, d], xrecv.at[j, d], (g, inward, c))

    def across(item, shard, d, part):
        i, there = item[0] + item[1], spot(item, shard, part)
        return remote(
            there,
            there,
            ysend.at[i, shard, d],
            yrecv.at[i, shard, d],
            (lax.rem(g + d, groups), s, c),
        )

    def write_up(shard, own=False):
        there = all_writes.at[shard, :, mine]
        return remote(
            writes if own else there, there, wsend.at[shard], wrecv.at[shard], (g, s + 1, c)
        )

    def write_peer(shard, d, origin):
        there = all_writes.at[shard, :, lanes(origin, wide)]
        return remote(
            there,
            there,
            psend.at[shard, d],
            precv.at[shard, d],
            (g, s, lax.rem(c + d, sections)),
        )

    def pull_near():
        return remote(up_far, ups.at[g], usend.at[0], urecv.at[g], (owner, s, c))

    def pull_far():
        at = groups + g
        return remote(up_far, ups.at[at], usend.at[0], urecv.at[at], (owner, inward, c))

    def give_back(j, u, where):
        return remote(
            dmixed_out.at[j, u],
            dmixed.at[j],
            dsend.at[j, u],
            drecv.at[j],
            (lax.rem(u, groups), where, c),
        )

    def own_copy(w):
        src, dst = ((w_kv, all_kv), (w_o, all_o), (w_q, all_q))[w]
        return pltpu.make_async_copy(src, dst.at[lanes(s, src.shape[0]), :], local.at[w])

    def rises(kind):
        return (owns & (s > 0) & (s < n - 2)) | (owns & first) if kind == O else s < n - 1

    def falls(kind):
        return (owns & (s < n - 1) & (s > 1)) | (owns & last) if kind == O else s > 0

    def skips(kind, shard):
        if kind != Q:
            return shard < 0
        return ((shard == 0) & (s == 1)) | ((shard == n - 1) & (s == n - 2))

    def pieces(kind):
        return [(kind, k) for k in range(PIECES[kind])]

    rising = list(reversed(pieces(Q)))

    def start_own(kind):
        for fall in pieces(kind):
            rise = (kind, CHUNKS - 1 - fall[1]) if kind == Q else fall

            @pl.when(rises(kind))
            def _():
                up(rise, s, True).start()

            @pl.when(falls(kind))
            def _():
                down(fall, s, True).start()

    def spread(item, shard):
        if item[0] == O:
            return

        def send():
            for d in range(1, groups):
                across(item, shard, d, g).start()

        if item[0] == KV:
            send()
        else:
            pl.when(jnp.logical_not(skips(Q, shard)))(send)

    def from_below(item, shard):
        up(item, shard).wait_recv()

        @pl.when(rises(item[0]))
        def _():
            up(item, shard).start()

        spread(item, shard)

    def from_above(item, shard):
        down(item, shard).wait_recv()

        @pl.when(falls(item[0]))
        def _():
            down(item, shard).start()

        spread(item, shard)

    def reaches(kind):
        return owns & inner if kind == O else s >= 0

    def serve(kind, k, inside=False):
        low = 1 if inside else 0

        @pl.when((s - k >= low) & reaches(kind))
        def _():
            for item in rising if kind == Q else pieces(kind):
                from_below(item, s - k)

        @pl.when((s + k < n - low) & reaches(kind))
        def _():
            for item in pieces(kind):
                from_above(item, s + k)

    def finish(item):
        @pl.loop(0, n)
        def _(shard):
            skipped = skips(item[0], shard)

            @pl.when((shard != s) & jnp.logical_not(skipped))
            def _():
                for d in range(1, groups):
                    across(item, shard, d, lax.rem(g + groups - d, groups)).wait_recv()

            if item[0] == Q:

                @pl.when(skipped)
                def _():
                    for d in range(1, groups):
                        extra(item[1], d, shard).wait_recv()

    def drain(item):
        kind = item[0]

        @pl.loop(0, n)
        def _(shard):
            if kind != O:

                @pl.when((shard != s) & jnp.logical_not(skips(kind, shard)))
                def _():
                    for d in range(1, groups):
                        across(item, shard, d, g).wait_send()

            @pl.when((shard <= s) & rises(kind))
            def _():
                up(item, shard).wait_send()

            @pl.when((shard >= s) & falls(kind))
            def _():
                down(item, shard).wait_send()

    @pl.when(s < n - 1)
    def _():
        write_up(s, True).start()

    start_own(KV)

    @pl.when(inner & jnp.logical_not(owns))
    def _():
        pull_near().start()

    @pl.when(end & jnp.logical_not(owns))
    def _():
        pull_far().start()

    pl.when(first)(lambda: start_own(Q))
    start_own(O)
    pl.when(s > 0)(lambda: start_own(Q))

    @pl.when(end & owns)
    def _():
        pull_far().start()

    @pl.when(end)
    def _():
        for j in range(CHUNKS):
            for d in range(1, groups):
                extra(j, d, s, True).start()

    for w in range(3):
        own_copy(w).start()

    strip = 32

    def norm_rows(from_ref, to_row):
        @pl.loop(0, from_ref.shape[0] // strip)
        def _(r):
            x = from_ref[lanes(r, strip), :].astype(f32)
            scale = lax.rsqrt(jnp.mean(x * x, axis=-1, keepdims=True) + epsilon)
            to = pl.ds(pl.multiple_of(to_row + r * strip, strip), strip)
            normed[to, :] = (x * scale * gain[...]).astype(bf16)
            scales[to, :] = scale

    input_copy(0).wait()
    input_copy(1).wait()
    norm_rows(rows_in, MEM)

    whole_gate = gate[...]
    high = whole_gate.astype(bf16)
    rest = whole_gate - high.astype(f32)
    middle = rest.astype(bf16)
    gates[0] = high
    gates[1] = middle
    gates[2] = (rest - middle.astype(f32)).astype(bf16)

    keyed = lax.broadcasted_iota(jnp.int32, (BLK, BLK), 0)
    asked = lax.broadcasted_iota(jnp.int32, (BLK, BLK), 1)
    blocks = count // BLK
    for b in range(blocks):
        seen = jnp.where(pattern[b, 0] > 0, 0.0, masked_score)
        parts = [jnp.full((MEM, BLK), seen, f32)]
        for e in range(b):
            seen = jnp.where(pattern[b, 1 + e] > 0, 0.0, masked_score)
            parts.append(jnp.full((BLK, BLK), seen, f32))
        parts.append(jnp.where(keyed <= asked, 0.0, masked_score).astype(f32))
        for e, part in enumerate(parts):
            for r in range(PAIR):
                bias[b, e * BLK : (e + 1) * BLK, r * BLK : (r + 1) * BLK] = part

    state[...] = jnp.zeros_like(state)
    passed[...] = jnp.ones_like(passed)
    cut = width // HEADS

    def serve_writes(k):
        @pl.when(s - k >= 0)
        def _():
            write_up(s - k).wait_recv()

            @pl.when(s < n - 1)
            def _():
                write_up(s - k).start()

            for d in range(1, sections):
                write_peer(s - k, d, c).start()

    def add_writes(k):
        @pl.when(s - k >= 0)
        def _():
            for d in range(1, sections):
                write_peer(s - k, d, lax.rem(c + sections - d, sections)).wait_recv()
            w = all_writes[s - k]
            logits = sum(
                lax.dot_general(w, gates[p], NT, preferred_element_type=f32) for p in range(3)
            )
            keep = jax.nn.sigmoid(logits + gate_bias[...])
            fresh = passed[...] * (1.0 - keep)
            passed[...] = passed[...] * keep
            for h in range(HEADS):
                at = slice(h * cut, (h + 1) * cut)
                state[:, at] += fresh[:, h : h + 1] * w[:, at].astype(f32)

    def turn(t):
        return jnp.where(s < n // 2, t, CHUNKS - 1 - t)

    def sent_far(j):
        return (j != far) if native else (j >= 0)

    def give_all(t, away):
        j = turn(t)
        base = groups if away else 0
        weight = all_o[lanes(j, span), :]
        pulled = ups[base : base + groups].reshape(groups * count, width)
        part = lax.dot_general(pulled, weight, NT, preferred_element_type=f32).astype(bf16)
        for u in range(groups):
            piece = part[u * count : (u + 1) * count]
            dmixed_out[j, base + u] = piece
            if away:

                @pl.when(sent_far(j))
                def _():
                    give_back(j, base + u, far).start()

            else:

                @pl.when(u == g)
                def _():
                    dmixed[j] = piece

                @pl.when(u != g)
                def _():
                    give_back(j, u, s).start()

    def project(t):
        pl.when(owns & inner)(lambda: give_all(t, False))

    def project_far(t):
        pl.when(owns & near_end)(lambda: give_all(t, True))

    beyond = (lax.rem(g + 1, groups), s, c)

    def wait_pulls(low, high):
        @pl.loop(low, high)
        def _(u):
            @pl.when(u != g)
            def _():
                remote(up_far, ups.at[u], usend.at[0], urecv.at[u], beyond).wait_recv()

    def ready_near():
        @pl.when(owns & inner)
        def _():
            own_copy(1).wait()
            wait_pulls(0, groups)

    def ready_far():
        @pl.when(owns & near_end)
        def _():
            wait_pulls(groups, 2 * groups)

    def at(where, steps, among=None):
        who = s == where
        if among is not None:
            who = who & (owns if among else jnp.logical_not(owns))

        @pl.when(who)
        def _():
            for item, shard in steps:
                if shard < where:
                    from_below(item, shard)
                else:
                    from_above(item, shard)

    def all_of(items, *shards):
        return [(item, shard) for item in items for shard in shards]

    if n == 4:
        kvs, qs, os = pieces(KV), pieces(Q), pieces(O)
        serve_writes(1)
        at(0, all_of(kvs, 1))
        at(1, all_of(kvs, 2, 0))
        at(2, all_of(kvs, 3, 1))
        at(3, all_of(kvs, 2))
        add_writes(1)
        at(0, all_of(qs, 1))
        ups_0, downs_2, o_0, o_2 = (
            all_of(rising, 0),
            all_of(qs, 2),
            all_of(os, 0),
            all_of(os, 2),
        )
        at(
            1,
            o_2[:1]
            + ups_0[:2]
            + o_2[1:2]
            + ups_0[2:]
            + o_2[2:3]
            + o_0[:1]
            + o_2[3:]
            + downs_2[:3]
            + o_0[1:2]
            + downs_2[3:],
            True,
        )
        at(1, downs_2, False)
        ups_1, downs_3 = all_of(rising, 1), all_of(qs, 3)
        at(
            2,
            all_of(os, 3, 1)
            + downs_3[:1]
            + ups_1[:3]
            + downs_3[1:2]
            + ups_1[3:]
            + downs_3[2:3],
            True,
        )
        at(2, ups_1, False)
        at(3, all_of(rising, 2))
        serve_writes(2)
        at(0, all_of(kvs, 2))
        at(1, all_of(kvs, 3))
        at(1, o_0[2:3], True)
        at(2, downs_3[3:], True)
        at(2, all_of(kvs, 0))
        at(3, all_of(kvs, 1))
        add_writes(2)
        at(0, all_of(qs, 2) + all_of(kvs, 3))
        at(1, all_of(os, 3)[:1] + o_0[3:], True)
        mixed_steps = [step for pair in zip(ups_0, downs_3) for step in pair]
        at(1, mixed_steps, False)
        at(2, ups_0, True)
        at(2, downs_3[:3] + ups_0[:1] + downs_3[3:] + ups_0[1:], False)
        at(3, all_of(rising, 1))
        serve_writes(3)
        at(3, all_of(kvs, 0))
        ready_near()
        for t in range(3):
            project(t)
        add_writes(3)
    else:

        @pl.loop(1, n)
        def _(k):
            serve_writes(k)
            serve(KV, k)
            serve(O, k)
            serve(Q, k, True)
            add_writes(k)

        ready_near()
        for t in range(CHUNKS):
            project(t)
        ready_far()
        for t in range(CHUNKS):
            project_far(t)

        @pl.when(inner)
        def _():
            for fall, rise in zip(pieces(Q), rising):
                from_below(rise, 0)
                from_above(fall, n - 1)

    @pl.when(jnp.logical_not(owns & inner))
    def _():
        own_copy(1).wait()

        if native:

            @pl.when(end)
            def _():
                dmixed[s] = lax.dot_general(
                    ups[g], all_o[lanes(s, span), :], NT, preferred_element_type=f32
                ).astype(bf16)

    if n == 4:
        at(1, all_of(os, 3)[1:] + downs_3, True)

    memory[...] = state[...].astype(bf16)
    norm_rows(memory, 0)

    own_copy(0).wait()
    own_copy(2).wait()
    for item in pieces(KV):
        finish(item)
    for kind, to in ((0, keys), (1, values)):
        part = jnp.dot(
            normed[...], all_kv[:, kind * span : (kind + 1) * span], preferred_element_type=f32
        ).astype(bf16)
        for h in range(KV_HEADS):
            to[h] = part[:, h * HEAD : (h + 1) * HEAD]

    rowdots[...] = jnp.zeros_like(rowdots)

    if n == 4:
        at(2, o_0[:2], True)
        ready_far()
        project_far(1)
        project_far(2)
        at(2, o_0[2:], True)
        project(3)
        project_far(3)

    def attend(j):
        ready = owns & inner
        if native:
            ready = ready | (end & (j == s))

        @pl.when(jnp.logical_not(ready))
        def _():
            remote(
                dmixed_out.at[j, 0], dmixed.at[j], dsend.at[j, 0], drecv.at[j], beyond
            ).wait_recv()

        queries = jnp.dot(
            normed[MEM:, :], all_q[:, lanes(j, span)], preferred_element_type=f32
        ).astype(bf16)
        small = (queries.astype(f32) * HEAD ** (-0.5)).astype(bf16)
        key, value = keys[j], values[j]
        small_key = (key.astype(f32) * HEAD ** (-0.5)).astype(bf16)
        pulled = dmixed[j]
        dkey = [jnp.zeros((BLK, HEAD), f32) for _ in range(blocks + 1)]
        dvalue = [jnp.zeros((BLK, HEAD), f32) for _ in range(blocks + 1)]
        dquery = [[None] * blocks for _ in range(GROUP)]
        for h in range(0, GROUP, PAIR):
            for b in range(blocks):
                rows = slice(b * BLK, (b + 1) * BLK)
                depth = MEM + (b + 1) * BLK

                def stacked(x):
                    return jnp.concatenate(
                        [x[rows, (h + r) * HEAD : (h + r + 1) * HEAD] for r in range(PAIR)], axis=0
                    )

                query, dhead = stacked(small), stacked(pulled)
                scores = lax.dot_general(key[:depth], query, NT, preferred_element_type=f32)
                scores = scores + bias[b, :depth, :]
                raised = jnp.exp(scores - jnp.max(scores, axis=0, keepdims=True))
                probs = raised * (1.0 / jnp.sum(raised, axis=0, keepdims=True))
                dprobs = lax.dot_general(value[:depth], dhead, NT, preferred_element_type=f32)
                drop = jnp.sum(probs * dprobs, axis=0, keepdims=True)
                dscores = (probs * (dprobs - drop)).astype(bf16)
                dv = jnp.dot(probs.astype(bf16), dhead, preferred_element_type=f32)
                dk = jnp.dot(dscores, query, preferred_element_type=f32)
                for e in range(depth // BLK):
                    dvalue[e] += dv[e * BLK : (e + 1) * BLK]
                    dkey[e] += dk[e * BLK : (e + 1) * BLK]
                back = lax.dot_general(small_key[:depth], dscores, TN, preferred_element_type=f32)
                for r in range(PAIR):
                    dquery[h + r][b] = back[:, r * BLK : (r + 1) * BLK]
        dquery = [jnp.concatenate(parts, axis=1) for parts in dquery]
        dkey = jnp.concatenate(dkey, axis=0)
        dvalue = jnp.concatenate(dvalue, axis=0)
        dkey = dkey.astype(bf16)
        dvalue = dvalue.astype(bf16)
        dkeys[j] = dkey
        dvalues[j] = dvalue
        dquery = jnp.concatenate(dquery, axis=0).T.astype(bf16)
        dq[:, lanes(j, span)] = dquery
        rowdots[...] += jnp.sum(
            dkey.astype(f32) * key.astype(f32) + dvalue.astype(f32) * value.astype(f32),
            axis=-1,
            keepdims=True,
        )
        rowdots[MEM:, :] += jnp.sum(
            dquery.astype(f32) * queries.astype(f32), axis=-1, keepdims=True
        )

    def serve_end(t):
        j = turn(t)

        @pl.when(last)
        def _():
            from_below((Q, j), 0)

        @pl.when(first)
        def _():
            from_above((Q, j), n - 1)

    serve_end(0)
    serve_end(1)
    for t in range(CHUNKS):
        if t == 1:
            for later in range(2, CHUNKS):
                serve_end(later)
        j = turn(t)
        finish((Q, j))
        attend(j)

    dkv = jnp.concatenate(
        [dkeys[h] for h in range(KV_HEADS)] + [dvalues[h] for h in range(KV_HEADS)], axis=1
    )
    tile = 256
    scale = scales[...]
    coef = rowdots[...] * scale * scale * (1.0 / width)

    def leaving(t):
        at = lanes(t, tile)
        return (
            pltpu.make_async_copy(grad_rows.at[:, at], out_rows.at[:, at], leave.at[0, t]),
            pltpu.make_async_copy(grad_memory.at[:, at], out_memory.at[:, at], leave.at[1, t]),
        )

    @pl.loop(0, width // tile, unroll=8)
    def _(t):
        at = lanes(t, tile)
        both = lax.dot_general(dkv, all_kv[at, :], NT, preferred_element_type=f32)
        ones = lax.dot_general(dq[...], all_q[at, :], NT, preferred_element_type=f32)
        strength = gain[:, at]
        grad_memory[:, at] = (
            both[:MEM] * strength * scale[:MEM] - memory[:, at].astype(f32) * coef[:MEM]
        ).astype(bf16)
        grad_rows[:, at] = (
            (both[MEM:] + ones) * strength * scale[MEM:]
            - rows_in[:, at].astype(f32) * coef[MEM:]
            + ups[g, :, at].astype(f32)
        ).astype(bf16)
        for copy in leaving(t):
            copy.start()

    @pl.loop(0, n)
    def _(shard):
        @pl.when(shard < s)
        def _():
            for d in range(1, sections):
                write_peer(shard, d, c).wait_send()

        @pl.when((shard <= s) & (s < n - 1))
        def _():
            write_up(shard).wait_send()

    for kind in PIECES:
        for item in pieces(kind):
            drain(item)

    @pl.when(end)
    def _():
        pull_far().wait_send()
        for j in range(CHUNKS):
            for d in range(1, groups):
                extra(j, d, s, True).wait_send()

    @pl.when(inner & jnp.logical_not(owns))
    def _():
        pull_near().wait_send()

    @pl.loop(0, width // tile)
    def _(t):
        for copy in leaving(t):
            copy.wait()

    @pl.when(inner & owns)
    def _():
        @pl.loop(0, CHUNKS)
        def _(j):
            @pl.loop(0, 2 * groups)
            def _(u):
                @pl.when((u < groups) & (u != g))
                def _():
                    give_back(j, u, s).wait_send()

                @pl.when((u >= groups) & near_end & sent_far(j))
                def _():
                    give_back(j, u, far).wait_send()


def hand_over(rows_from, memory_from, rows_to, memory_to, rows, memory, sems):
    cut = memory_from.shape[0] // 2

    def moves(k, src, dst, w, way):
        at = slice(k * cut, (k + 1) * cut)
        return pltpu.make_async_copy(src.at[at, :], dst.at[at, :], sems.at[way, w, k])

    pairs = ((rows_from, rows, rows_to), (memory_from, memory, memory_to))
    spans = [(w, k) for w in range(2) for k in range(pairs[w][0].shape[0] // cut)]
    for w, k in spans:
        moves(k, pairs[w][0], pairs[w][1], w, 0).start()
    for w, k in spans:
        moves(k, pairs[w][0], pairs[w][1], w, 0).wait()
        moves(k, pairs[w][1], pairs[w][2], w, 1).start()
    for w, k in spans:
        moves(k, pairs[w][1], pairs[w][2], w, 1).wait()


def per_device(
    n,
    groups,
    sections,
    writes,
    layer_inputs,
    upstream,
    pattern,
    w_q,
    w_kv,
    w_o,
    norm_gain,
    gate_weight,
    gate_bias,
):
    count, width = layer_inputs.shape[2:]
    total = MEM + count
    span = HEADS * HEAD // CHUNKS
    anywhere = pl.BlockSpec(memory_space=pl.ANY)
    near = pl.BlockSpec(memory_space=pltpu.VMEM)
    dma = pltpu.SemaphoreType.DMA
    bf16, f32 = jnp.bfloat16, jnp.float32
    grads = pl.pallas_call(
        functools.partial(layer_kernel, n, groups, sections),
        out_shape=[
            jax.ShapeDtypeStruct((count, width), bf16),
            jax.ShapeDtypeStruct((MEM, width), bf16),
        ],
        in_specs=[pl.BlockSpec(memory_space=pltpu.SMEM), anywhere, anywhere, anywhere]
        + [near] * 3
        + [anywhere] * 3,
        out_specs=[anywhere, anywhere],
        scratch_shapes=[
            pltpu.VMEM((count, width), bf16),
            pltpu.VMEM((MEM, width), bf16),
            pltpu.VMEM((count, width), bf16),
            pltpu.VMEM((2 * groups, count, width), bf16),
            pltpu.VMEM((n, MEM, width), bf16),
            pltpu.VMEM((width, w_kv.shape[2]), bf16),
            pltpu.VMEM((width, HEADS * HEAD), bf16),
            pltpu.VMEM((HEADS * HEAD, width), bf16),
            pltpu.VMEM((total, width), bf16),
            pltpu.VMEM((total, 1), f32),
            pltpu.VMEM((MEM, width), bf16),
            pltpu.VMEM((MEM, width), f32),
            pltpu.VMEM((MEM, HEADS), f32),
            pltpu.VMEM((3, HEADS, width), bf16),
            pltpu.VMEM((KV_HEADS, total, HEAD), bf16),
            pltpu.VMEM((KV_HEADS, total, HEAD), bf16),
            pltpu.VMEM((count // BLK, total, PAIR * BLK), f32),
            pltpu.VMEM((KV_HEADS, count, span), bf16),
            pltpu.VMEM((KV_HEADS, 2 * groups, count, span), bf16),
            pltpu.VMEM((count, HEADS * HEAD), bf16),
            pltpu.VMEM((KV_HEADS, total, HEAD), bf16),
            pltpu.VMEM((KV_HEADS, total, HEAD), bf16),
            pltpu.VMEM((total, 1), f32),
            dma((ITEMS, n)),
            dma((ITEMS, n)),
            dma((ITEMS, n)),
            dma((CHUNKS, groups)),
            dma((CHUNKS, groups)),
            dma((O, n, groups)),
            dma((O, n, groups)),
            dma((n,)),
            dma((n,)),
            dma((n, sections)),
            dma((n, sections)),
            dma((1,)),
            dma((2 * groups,)),
            dma((CHUNKS, 2 * groups)),
            dma((CHUNKS,)),
            dma((5,)),
            dma((2, width // 256)),
        ],
        compiler_params=pltpu.CompilerParams(
            collective_id=0, has_side_effects=True, vmem_limit_bytes=56 * 1024 * 1024
        ),
    )(
        pattern[0],
        writes[0],
        layer_inputs[0, 0],
        upstream[0, 0],
        norm_gain,
        gate_weight[0].T,
        gate_bias,
        w_kv[0],
        w_q[0],
        w_o[0],
    )
    grads = pl.pallas_call(
        hand_over,
        out_shape=[
            jax.ShapeDtypeStruct((count, width), bf16),
            jax.ShapeDtypeStruct((MEM, width), bf16),
        ],
        in_specs=[anywhere, anywhere],
        out_specs=[anywhere, anywhere],
        scratch_shapes=[
            pltpu.VMEM((count, width), bf16),
            pltpu.VMEM((MEM, width), bf16),
            dma((2, 2, 2 * count // MEM)),
        ],
    )(*grads)
    return (grads[0][None, None], grads[1][None, None])


def solution(mesh):
    placed = (
        P(("groups", "seg"), None, "section"),
        P("section", ("groups", "seg"), None, None),
        P("section", ("groups", "seg"), None, None),
        P(("groups", "seg"), None, None),
        P("section", "seg", None),
        P("section", "seg", None),
        P("section", "seg", None),
        P("section", None),
        P("section", None, None),
        P("section", None),
    )
    sizes = (mesh.shape["seg"], mesh.shape["groups"], mesh.shape["section"])
    return jax.shard_map(
        functools.partial(per_device, *sizes),
        mesh=mesh,
        in_specs=placed,
        out_specs=(
            P("section", ("groups", "seg"), None, None),
            P("section", ("groups", "seg"), None, None),
        ),
        check_vma=False,
    )
```

```python
import functools

import jax
import jax.numpy as jnp
from jax import lax
from jax.experimental import pallas as pl
from jax.experimental.pallas import tpu as pltpu
from jax.sharding import PartitionSpec as P

HEADS = 16
KV_HEADS = 4
HEAD = 64
BLK = 128
MEM = 128


epsilon = 1e-05
masked_score = -1e30
GROUP = HEADS // KV_HEADS
NT = (((1,), (1,)), ((), ()))
TN = (((0,), (0,)), ((), ()))
CHUNKS = KV_HEADS
PAIR = 2
STRIPS = 4
KV, Q, O = 0, PAIR, PAIR + CHUNKS
PIECES = {KV: PAIR, Q: CHUNKS, O: STRIPS}
ITEMS = PAIR + CHUNKS + STRIPS
MESH = pl.DeviceIdType.MESH


def layer_kernel(
    n,
    groups,
    sections,
    pattern,
    writes,
    rows_far,
    up_far,
    gain,
    gate,
    gate_bias,
    w_kv,
    w_q,
    w_o,
    out_rows,
    out_memory,
    grad_rows,
    grad_memory,
    rows_in,
    ups,
    all_writes,
    all_kv,
    all_q,
    all_o,
    normed,
    scales,
    memory,
    state,
    passed,
    gates,
    keys,
    values,
    bias,
    dmixed,
    dmixed_out,
    dq,
    dkeys,
    dvalues,
    rowdots,
    *sems,
):
    (
        up_sem,
        down_sem,
        zrecv,
        xsend,
        xrecv,
        ysend,
        yrecv,
        wsend,
        wrecv,
        psend,
        precv,
        usend,
        urecv,
        dsend,
        drecv,
        local,
        leave,
    ) = sems
    g = lax.axis_index("groups")
    s = lax.axis_index("seg")
    c = lax.axis_index("section")
    count, width = rows_in.shape
    wide = writes.shape[1]
    span = all_q.shape[1] // CHUNKS
    half_kv = all_kv.shape[1] // PAIR
    f32, bf16 = jnp.float32, jnp.bfloat16
    native = n == CHUNKS

    owner = lax.rem(c, groups)
    owns = g == owner
    first, last = s == 0, s == n - 1
    end = first | last
    inner = jnp.logical_not(end)
    near_end = (s == 1) | (s == n - 2)
    far = jnp.where(s == 1, 0, n - 1)
    inward = jnp.where(first, 1, n - 2)

    def lanes(at, size):
        return pl.ds(pl.multiple_of(at * size, size), size)

    mine = lanes(c, wide)

    barrier = pltpu.get_barrier_semaphore()

    def greet(where):
        pl.semaphore_signal(barrier, inc=1, device_id=where, device_id_type=MESH)

    @pl.when(s > 0)
    def _():
        greet((g, s - 1, c))

    @pl.when(s < n - 1)
    def _():
        greet((g, s + 1, c))

    for d in range(1, groups):
        greet((lax.rem(g + d, groups), s, c))

        @pl.when(end)
        def _():
            greet((lax.rem(g + d, groups), inward, c))

        @pl.when(near_end)
        def _():
            greet((lax.rem(g + d, groups), far, c))

    for d in range(1, sections):
        greet((g, s, lax.rem(c + d, sections)))

    def input_copy(k):
        if k == 0:
            return pltpu.make_async_copy(rows_far, rows_in, local.at[3])
        return pltpu.make_async_copy(up_far, ups.at[g], local.at[4])

    input_copy(0).start()
    input_copy(1).start()

    beside = jnp.where(end, 1, 2) + jnp.where(end | near_end, groups - 1, 0)
    pl.semaphore_wait(barrier, beside + groups + sections - 2)

    def remote(src, dst, send, recv, where):
        return pltpu.make_async_remote_copy(
            src_ref=src,
            dst_ref=dst,
            send_sem=send,
            recv_sem=recv,
            device_id=where,
            device_id_type=MESH,
        )

    def operand(kind):
        return {
            KV: (w_kv, all_kv, half_kv),
            Q: (w_q, all_q, span),
            O: (w_o, all_o, width // STRIPS),
        }[kind]

    def columns(kind, chunk):
        cols = operand(kind)[2]
        if isinstance(chunk, int):
            return slice(chunk * cols, (chunk + 1) * cols)
        return lanes(chunk, cols)

    def spot(item, shard, part):
        kind, chunk = item
        src, dst, _ = operand(kind)
        at = columns(kind, chunk)
        if kind == O:
            return dst.at[lanes(shard, src.shape[0]), at]
        half = src.shape[0] // groups
        return dst.at[lanes(shard * groups + part, half), at]

    def source(item, part):
        kind, chunk = item
        src = operand(kind)[0]
        at = columns(kind, chunk)
        if kind == O:
            return src.at[:, at]
        return src.at[lanes(part, src.shape[0] // groups), at]

    def up(item, shard, own=False):
        i, there = item[0] + item[1], spot(item, shard, g)
        src = source(item, g) if own else there
        return remote(src, there, up_sem.at[i, shard], zrecv.at[i, shard], (g, s + 1, c))

    def down(item, shard, own=False):
        i, there = item[0] + item[1], spot(item, shard, g)
        src = source(item, g) if own else there
        return remote(src, there, down_sem.at[i, shard], zrecv.at[i, shard], (g, s - 1, c))

    def extra(j, d, shard, own=False):
        part = lax.rem(g + d, groups)
        there = spot((Q, j), shard, part)
        src = source((Q, j), part) if own else there
        return remote(src, there, xsend.at[j, d], xrecv.at[j, d], (g, inward, c))

    def across(item, shard, d, part):
        i, there = item[0] + item[1], spot(item, shard, part)
        return remote(
            there,
            there,
            ysend.at[i, shard, d],
            yrecv.at[i, shard, d],
            (lax.rem(g + d, groups), s, c),
        )

    def write_up(shard, own=False):
        there = all_writes.at[shard, :, mine]
        return remote(
            writes if own else there, there, wsend.at[shard], wrecv.at[shard], (g, s + 1, c)
        )

    def write_peer(shard, d, origin):
        there = all_writes.at[shard, :, lanes(origin, wide)]
        return remote(
            there,
            there,
            psend.at[shard, d],
            precv.at[shard, d],
            (g, s, lax.rem(c + d, sections)),
        )

    def pull_near():
        return remote(up_far, ups.at[g], usend.at[0], urecv.at[g], (owner, s, c))

    def pull_far():
        at = groups + g
        return remote(up_far, ups.at[at], usend.at[0], urecv.at[at], (owner, inward, c))

    def give_back(j, u, where):
        return remote(
            dmixed_out.at[j, u],
            dmixed.at[j],
            dsend.at[j, u],
            drecv.at[j],
            (lax.rem(u, groups), where, c),
        )

    def own_copy(w):
        src, dst = ((w_kv, all_kv), (w_o, all_o), (w_q, all_q))[w]
        return pltpu.make_async_copy(src, dst.at[lanes(s, src.shape[0]), :], local.at[w])

    def rises(kind):
        return (owns & (s > 0) & (s < n - 2)) | (owns & first) if kind == O else s < n - 1

    def falls(kind):
        return (owns & (s < n - 1) & (s > 1)) | (owns & last) if kind == O else s > 0

    def skips(kind, shard):
        if kind != Q:
            return shard < 0
        return ((shard == 0) & (s == 1)) | ((shard == n - 1) & (s == n - 2))

    def pieces(kind):
        return [(kind, k) for k in range(PIECES[kind])]

    rising = list(reversed(pieces(Q)))

    def start_own(kind):
        for fall in pieces(kind):
            rise = (kind, CHUNKS - 1 - fall[1]) if kind == Q else fall

            @pl.when(rises(kind))
            def _():
                up(rise, s, True).start()

            @pl.when(falls(kind))
            def _():
                down(fall, s, True).start()

    def spread(item, shard):
        if item[0] == O:
            return

        def send():
            for d in range(1, groups):
                across(item, shard, d, g).start()

        if item[0] == KV:
            send()
        else:
            pl.when(jnp.logical_not(skips(Q, shard)))(send)

    def from_below(item, shard):
        up(item, shard).wait_recv()

        @pl.when(rises(item[0]))
        def _():
            up(item, shard).start()

        spread(item, shard)

    def from_above(item, shard):
        down(item, shard).wait_recv()

        @pl.when(falls(item[0]))
        def _():
            down(item, shard).start()

        spread(item, shard)

    def reaches(kind):
        return owns & inner if kind == O else s >= 0

    def serve(kind, k, inside=False):
        low = 1 if inside else 0

        @pl.when((s - k >= low) & reaches(kind))
        def _():
            for item in rising if kind == Q else pieces(kind):
                from_below(item, s - k)

        @pl.when((s + k < n - low) & reaches(kind))
        def _():
            for item in pieces(kind):
                from_above(item, s + k)

    def finish(item):
        @pl.loop(0, n)
        def _(shard):
            skipped = skips(item[0], shard)

            @pl.when((shard != s) & jnp.logical_not(skipped))
            def _():
                for d in range(1, groups):
                    across(item, shard, d, lax.rem(g + groups - d, groups)).wait_recv()

            if item[0] == Q:

                @pl.when(skipped)
                def _():
                    for d in range(1, groups):
                        extra(item[1], d, shard).wait_recv()

    def drain(item):
        kind = item[0]

        @pl.loop(0, n)
        def _(shard):
            if kind != O:

                @pl.when((shard != s) & jnp.logical_not(skips(kind, shard)))
                def _():
                    for d in range(1, groups):
                        across(item, shard, d, g).wait_send()

            @pl.when((shard <= s) & rises(kind))
            def _():
                up(item, shard).wait_send()

            @pl.when((shard >= s) & falls(kind))
            def _():
                down(item, shard).wait_send()

    @pl.when(s < n - 1)
    def _():
        write_up(s, True).start()

    start_own(KV)

    @pl.when(inner & jnp.logical_not(owns))
    def _():
        pull_near().start()

    @pl.when(end & jnp.logical_not(owns))
    def _():
        pull_far().start()

    pl.when(first)(lambda: start_own(Q))
    start_own(O)
    pl.when(s > 0)(lambda: start_own(Q))

    @pl.when(end & owns)
    def _():
        pull_far().start()

    for w in range(3):
        own_copy(w).start()

    strip = 32

    def norm_rows(from_ref, to_row):
        @pl.loop(0, from_ref.shape[0] // strip)
        def _(r):
            x = from_ref[lanes(r, strip), :].astype(f32)
            scale = lax.rsqrt(jnp.mean(x * x, axis=-1, keepdims=True) + epsilon)
            to = pl.ds(pl.multiple_of(to_row + r * strip, strip), strip)
            normed[to, :] = (x * scale * gain[...]).astype(bf16)
            scales[to, :] = scale

    input_copy(0).wait()
    input_copy(1).wait()
    norm_rows(rows_in, MEM)

    whole_gate = gate[...]
    high = whole_gate.astype(bf16)
    rest = whole_gate - high.astype(f32)
    middle = rest.astype(bf16)
    gates[0] = high
    gates[1] = middle
    gates[2] = (rest - middle.astype(f32)).astype(bf16)

    keyed = lax.broadcasted_iota(jnp.int32, (BLK, BLK), 0)
    asked = lax.broadcasted_iota(jnp.int32, (BLK, BLK), 1)
    blocks = count // BLK
    for b in range(blocks):
        seen = jnp.where(pattern[b, 0] > 0, 0.0, masked_score)
        parts = [jnp.full((MEM, BLK), seen, f32)]
        for e in range(b):
            seen = jnp.where(pattern[b, 1 + e] > 0, 0.0, masked_score)
            parts.append(jnp.full((BLK, BLK), seen, f32))
        parts.append(jnp.where(keyed <= asked, 0.0, masked_score).astype(f32))
        for e, part in enumerate(parts):
            for r in range(PAIR):
                bias[b, e * BLK : (e + 1) * BLK, r * BLK : (r + 1) * BLK] = part

    state[...] = jnp.zeros_like(state)
    passed[...] = jnp.ones_like(passed)
    cut = width // HEADS

    def serve_writes(k):
        @pl.when(s - k >= 0)
        def _():
            write_up(s - k).wait_recv()

            @pl.when(s < n - 1)
            def _():
                write_up(s - k).start()

            for d in range(1, sections):
                write_peer(s - k, d, c).start()

    def add_writes(k):
        @pl.when(s - k >= 0)
        def _():
            for d in range(1, sections):
                write_peer(s - k, d, lax.rem(c + sections - d, sections)).wait_recv()
            w = all_writes[s - k]
            logits = sum(
                lax.dot_general(w, gates[p], NT, preferred_element_type=f32) for p in range(3)
            )
            keep = jax.nn.sigmoid(logits + gate_bias[...])
            fresh = passed[...] * (1.0 - keep)
            passed[...] = passed[...] * keep
            for h in range(HEADS):
                at = slice(h * cut, (h + 1) * cut)
                state[:, at] += fresh[:, h : h + 1] * w[:, at].astype(f32)

    def turn(t):
        return jnp.where(s < n // 2, t, CHUNKS - 1 - t)

    def sent_far(j):
        return (j != far) if native else (j >= 0)

    def give_all(t, away):
        j = turn(t)
        base = groups if away else 0
        weight = all_o[lanes(j, span), :]
        pulled = ups[base : base + groups].reshape(groups * count, width)
        part = lax.dot_general(pulled, weight, NT, preferred_element_type=f32).astype(bf16)
        for u in range(groups):
            piece = part[u * count : (u + 1) * count]
            dmixed_out[j, base + u] = piece
            if away:

                @pl.when(sent_far(j))
                def _():
                    give_back(j, base + u, far).start()

            else:

                @pl.when(u == g)
                def _():
                    dmixed[j] = piece

                @pl.when(u != g)
                def _():
                    give_back(j, u, s).start()

    def project(t):
        pl.when(owns & inner)(lambda: give_all(t, False))

    def project_far(t):
        pl.when(owns & near_end)(lambda: give_all(t, True))

    beyond = (lax.rem(g + 1, groups), s, c)

    def wait_pulls(low, high):
        @pl.loop(low, high)
        def _(u):
            @pl.when(u != g)
            def _():
                remote(up_far, ups.at[u], usend.at[0], urecv.at[u], beyond).wait_recv()

    def ready_near():
        @pl.when(owns & inner)
        def _():
            own_copy(1).wait()
            wait_pulls(0, groups)

    def ready_far():
        @pl.when(owns & near_end)
        def _():
            wait_pulls(groups, 2 * groups)

    def at(where, steps, among=None):
        who = s == where
        if among is not None:
            who = who & (owns if among else jnp.logical_not(owns))

        @pl.when(who)
        def _():
            for item, shard in steps:
                if shard < where:
                    from_below(item, shard)
                else:
                    from_above(item, shard)

    def all_of(items, *shards):
        return [(item, shard) for item in items for shard in shards]

    if n == 4:
        kvs, qs, os = pieces(KV), pieces(Q), pieces(O)
        serve_writes(1)
        at(0, all_of(kvs, 1))
        at(1, all_of(kvs, 2, 0))
        at(2, all_of(kvs, 3, 1))
        at(3, all_of(kvs, 2))
        add_writes(1)
        at(0, all_of(qs, 1))
        ups_0, downs_2, o_0, o_2 = (
            all_of(rising, 0),
            all_of(qs, 2),
            all_of(os, 0),
            all_of(os, 2),
        )
        at(
            1,
            o_2[:1]
            + ups_0[:2]
            + o_2[1:2]
            + ups_0[2:]
            + o_2[2:3]
            + o_0[:1]
            + o_2[3:]
            + downs_2[:3]
            + o_0[1:2]
            + downs_2[3:],
            True,
        )
        at(1, downs_2, False)
        ups_1, downs_3 = all_of(rising, 1), all_of(qs, 3)
        at(
            2,
            all_of(os, 3, 1)
            + downs_3[:1]
            + ups_1[:3]
            + downs_3[1:2]
            + ups_1[3:]
            + downs_3[2:3],
            True,
        )
        at(2, ups_1, False)
        at(3, all_of(rising, 2))
        serve_writes(2)
        at(0, all_of(kvs, 2))
        at(1, all_of(kvs, 3))
        at(1, o_0[2:3], True)
        at(2, downs_3[3:], True)
        at(2, all_of(kvs, 0))
        at(3, all_of(kvs, 1))
        add_writes(2)
        at(0, all_of(qs, 2) + all_of(kvs, 3))
        at(1, all_of(os, 3)[:1] + o_0[3:], True)
        mixed_steps = [step for pair in zip(ups_0, downs_3) for step in pair]
        at(1, mixed_steps, False)
        at(2, ups_0, True)
        at(2, downs_3[:3] + ups_0[:1] + downs_3[3:] + ups_0[1:], False)
        at(3, all_of(rising, 1))
        serve_writes(3)
        at(3, all_of(kvs, 0))
        @pl.when(end)
        def _():
            for j in range(CHUNKS):
                for d in range(1, groups):
                    extra(j, d, s, True).start()

        ready_near()
        for t in range(3):
            project(t)
        add_writes(3)
    else:

        @pl.loop(1, n)
        def _(k):
            serve_writes(k)
            serve(KV, k)
            serve(O, k)
            serve(Q, k, True)
            add_writes(k)

        @pl.when(end)
        def _():
            for j in range(CHUNKS):
                for d in range(1, groups):
                    extra(j, d, s, True).start()

        ready_near()
        for t in range(CHUNKS):
            project(t)
        ready_far()
        for t in range(CHUNKS):
            project_far(t)

        @pl.when(inner)
        def _():
            for fall, rise in zip(pieces(Q), rising):
                from_below(rise, 0)
                from_above(fall, n - 1)

    @pl.when(jnp.logical_not(owns & inner))
    def _():
        own_copy(1).wait()

        if native:

            @pl.when(end)
            def _():
                dmixed[s] = lax.dot_general(
                    ups[g], all_o[lanes(s, span), :], NT, preferred_element_type=f32
                ).astype(bf16)

    if n == 4:
        at(1, all_of(os, 3)[1:] + downs_3, True)

    memory[...] = state[...].astype(bf16)
    norm_rows(memory, 0)

    own_copy(0).wait()
    own_copy(2).wait()
    for item in pieces(KV):
        finish(item)
    for kind, to in ((0, keys), (1, values)):
        part = jnp.dot(
            normed[...], all_kv[:, kind * span : (kind + 1) * span], preferred_element_type=f32
        ).astype(bf16)
        for h in range(KV_HEADS):
            to[h] = part[:, h * HEAD : (h + 1) * HEAD]

    rowdots[...] = jnp.zeros_like(rowdots)

    if n == 4:
        at(2, o_0[:1], True)
        ready_far()
        project_far(1)
        project_far(2)
        at(2, o_0[1:], True)
        project(3)
        project_far(3)

    def attend(j):
        ready = owns & inner
        if native:
            ready = ready | (end & (j == s))

        @pl.when(jnp.logical_not(ready))
        def _():
            remote(
                dmixed_out.at[j, 0], dmixed.at[j], dsend.at[j, 0], drecv.at[j], beyond
            ).wait_recv()

        queries = jnp.dot(
            normed[MEM:, :], all_q[:, lanes(j, span)], preferred_element_type=f32
        ).astype(bf16)
        small = (queries.astype(f32) * HEAD ** (-0.5)).astype(bf16)
        key, value = keys[j], values[j]
        small_key = (key.astype(f32) * HEAD ** (-0.5)).astype(bf16)
        pulled = dmixed[j]
        dkey = [jnp.zeros((BLK, HEAD), f32) for _ in range(blocks + 1)]
        dvalue = [jnp.zeros((BLK, HEAD), f32) for _ in range(blocks + 1)]
        dquery = [[None] * blocks for _ in range(GROUP)]
        for h in range(0, GROUP, PAIR):
            for b in range(blocks):
                rows = slice(b * BLK, (b + 1) * BLK)
                depth = MEM + (b + 1) * BLK

                def stacked(x):
                    return jnp.concatenate(
                        [x[rows, (h + r) * HEAD : (h + r + 1) * HEAD] for r in range(PAIR)], axis=0
                    )

                query, dhead = stacked(small), stacked(pulled)
                scores = lax.dot_general(key[:depth], query, NT, preferred_element_type=f32)
                scores = scores + bias[b, :depth, :]
                raised = jnp.exp(scores - jnp.max(scores, axis=0, keepdims=True))
                probs = raised * (1.0 / jnp.sum(raised, axis=0, keepdims=True))
                dprobs = lax.dot_general(value[:depth], dhead, NT, preferred_element_type=f32)
                drop = jnp.sum(probs * dprobs, axis=0, keepdims=True)
                dscores = (probs * (dprobs - drop)).astype(bf16)
                dv = jnp.dot(probs.astype(bf16), dhead, preferred_element_type=f32)
                dk = jnp.dot(dscores, query, preferred_element_type=f32)
                for e in range(depth // BLK):
                    dvalue[e] += dv[e * BLK : (e + 1) * BLK]
                    dkey[e] += dk[e * BLK : (e + 1) * BLK]
                back = lax.dot_general(small_key[:depth], dscores, TN, preferred_element_type=f32)
                for r in range(PAIR):
                    dquery[h + r][b] = back[:, r * BLK : (r + 1) * BLK]
        dquery = [jnp.concatenate(parts, axis=1) for parts in dquery]
        dkey = jnp.concatenate(dkey, axis=0)
        dvalue = jnp.concatenate(dvalue, axis=0)
        dkey = dkey.astype(bf16)
        dvalue = dvalue.astype(bf16)
        dkeys[j] = dkey
        dvalues[j] = dvalue
        dquery = jnp.concatenate(dquery, axis=0).T.astype(bf16)
        dq[:, lanes(j, span)] = dquery
        rowdots[...] += jnp.sum(
            dkey.astype(f32) * key.astype(f32) + dvalue.astype(f32) * value.astype(f32),
            axis=-1,
            keepdims=True,
        )
        rowdots[MEM:, :] += jnp.sum(
            dquery.astype(f32) * queries.astype(f32), axis=-1, keepdims=True
        )

    def serve_end(t):
        j = turn(t)

        @pl.when(last)
        def _():
            from_below((Q, j), 0)

        @pl.when(first)
        def _():
            from_above((Q, j), n - 1)

    serve_end(0)
    serve_end(1)
    for t in range(CHUNKS):
        if t == 1:
            for later in range(2, CHUNKS):
                serve_end(later)
        j = turn(t)
        finish((Q, j))
        attend(j)

    dkv = jnp.concatenate(
        [dkeys[h] for h in range(KV_HEADS)] + [dvalues[h] for h in range(KV_HEADS)], axis=1
    )
    tile = 512
    scale = scales[...]
    coef = rowdots[...] * scale * scale * (1.0 / width)

    def leaving(t):
        at = lanes(t, tile)
        return (
            pltpu.make_async_copy(grad_rows.at[:, at], out_rows.at[:, at], leave.at[0, t]),
            pltpu.make_async_copy(grad_memory.at[:, at], out_memory.at[:, at], leave.at[1, t]),
        )

    @pl.loop(0, width // tile, unroll=4)
    def _(t):
        at = lanes(t, tile)
        both = lax.dot_general(dkv, all_kv[at, :], NT, preferred_element_type=f32)
        ones = lax.dot_general(dq[...], all_q[at, :], NT, preferred_element_type=f32)
        strength = gain[:, at]
        grad_memory[:, at] = (
            both[:MEM] * strength * scale[:MEM] - memory[:, at].astype(f32) * coef[:MEM]
        ).astype(bf16)
        grad_rows[:, at] = (
            (both[MEM:] + ones) * strength * scale[MEM:]
            - rows_in[:, at].astype(f32) * coef[MEM:]
            + ups[g, :, at].astype(f32)
        ).astype(bf16)
        for copy in leaving(t):
            copy.start()

    @pl.loop(0, n)
    def _(shard):
        @pl.when(shard < s)
        def _():
            for d in range(1, sections):
                write_peer(shard, d, c).wait_send()

        @pl.when((shard <= s) & (s < n - 1))
        def _():
            write_up(shard).wait_send()

    for kind in PIECES:
        for item in pieces(kind):
            drain(item)

    @pl.when(end)
    def _():
        pull_far().wait_send()
        for j in range(CHUNKS):
            for d in range(1, groups):
                extra(j, d, s, True).wait_send()

    @pl.when(inner & jnp.logical_not(owns))
    def _():
        pull_near().wait_send()

    @pl.loop(0, width // tile)
    def _(t):
        for copy in leaving(t):
            copy.wait()

    @pl.when(inner & owns)
    def _():
        @pl.loop(0, CHUNKS)
        def _(j):
            @pl.loop(0, 2 * groups)
            def _(u):
                @pl.when((u < groups) & (u != g))
                def _():
                    give_back(j, u, s).wait_send()

                @pl.when((u >= groups) & near_end & sent_far(j))
                def _():
                    give_back(j, u, far).wait_send()


def hand_over(rows_from, memory_from, rows_to, memory_to, rows, memory, sems):
    cut = memory_from.shape[0] // 2

    def moves(k, src, dst, w, way):
        at = slice(k * cut, (k + 1) * cut)
        return pltpu.make_async_copy(src.at[at, :], dst.at[at, :], sems.at[way, w, k])

    pairs = ((rows_from, rows, rows_to), (memory_from, memory, memory_to))
    spans = [(w, k) for w in range(2) for k in range(pairs[w][0].shape[0] // cut)]
    for w, k in spans:
        moves(k, pairs[w][0], pairs[w][1], w, 0).start()
    for w, k in spans:
        moves(k, pairs[w][0], pairs[w][1], w, 0).wait()
        moves(k, pairs[w][1], pairs[w][2], w, 1).start()
    for w, k in spans:
        moves(k, pairs[w][1], pairs[w][2], w, 1).wait()


def per_device(
    n,
    groups,
    sections,
    writes,
    layer_inputs,
    upstream,
    pattern,
    w_q,
    w_kv,
    w_o,
    norm_gain,
    gate_weight,
    gate_bias,
):
    count, width = layer_inputs.shape[2:]
    total = MEM + count
    span = HEADS * HEAD // CHUNKS
    anywhere = pl.BlockSpec(memory_space=pl.ANY)
    near = pl.BlockSpec(memory_space=pltpu.VMEM)
    dma = pltpu.SemaphoreType.DMA
    bf16, f32 = jnp.bfloat16, jnp.float32
    grads = pl.pallas_call(
        functools.partial(layer_kernel, n, groups, sections),
        out_shape=[
            jax.ShapeDtypeStruct((count, width), bf16),
            jax.ShapeDtypeStruct((MEM, width), bf16),
        ],
        in_specs=[pl.BlockSpec(memory_space=pltpu.SMEM), anywhere, anywhere, anywhere]
        + [near] * 3
        + [anywhere] * 3,
        out_specs=[anywhere, anywhere],
        scratch_shapes=[
            pltpu.VMEM((count, width), bf16),
            pltpu.VMEM((MEM, width), bf16),
            pltpu.VMEM((count, width), bf16),
            pltpu.VMEM((2 * groups, count, width), bf16),
            pltpu.VMEM((n, MEM, width), bf16),
            pltpu.VMEM((width, w_kv.shape[2]), bf16),
            pltpu.VMEM((width, HEADS * HEAD), bf16),
            pltpu.VMEM((HEADS * HEAD, width), bf16),
            pltpu.VMEM((total, width), bf16),
            pltpu.VMEM((total, 1), f32),
            pltpu.VMEM((MEM, width), bf16),
            pltpu.VMEM((MEM, width), f32),
            pltpu.VMEM((MEM, HEADS), f32),
            pltpu.VMEM((3, HEADS, width), bf16),
            pltpu.VMEM((KV_HEADS, total, HEAD), bf16),
            pltpu.VMEM((KV_HEADS, total, HEAD), bf16),
            pltpu.VMEM((count // BLK, total, PAIR * BLK), f32),
            pltpu.VMEM((KV_HEADS, count, span), bf16),
            pltpu.VMEM((KV_HEADS, 2 * groups, count, span), bf16),
            pltpu.VMEM((count, HEADS * HEAD), bf16),
            pltpu.VMEM((KV_HEADS, total, HEAD), bf16),
            pltpu.VMEM((KV_HEADS, total, HEAD), bf16),
            pltpu.VMEM((total, 1), f32),
            dma((ITEMS, n)),
            dma((ITEMS, n)),
            dma((ITEMS, n)),
            dma((CHUNKS, groups)),
            dma((CHUNKS, groups)),
            dma((O, n, groups)),
            dma((O, n, groups)),
            dma((n,)),
            dma((n,)),
            dma((n, sections)),
            dma((n, sections)),
            dma((1,)),
            dma((2 * groups,)),
            dma((CHUNKS, 2 * groups)),
            dma((CHUNKS,)),
            dma((5,)),
            dma((2, width // 512)),
        ],
        compiler_params=pltpu.CompilerParams(
            collective_id=0, has_side_effects=True, vmem_limit_bytes=56 * 1024 * 1024
        ),
    )(
        pattern[0],
        writes[0],
        layer_inputs[0, 0],
        upstream[0, 0],
        norm_gain,
        gate_weight[0].T,
        gate_bias,
        w_kv[0],
        w_q[0],
        w_o[0],
    )
    grads = pl.pallas_call(
        hand_over,
        out_shape=[
            jax.ShapeDtypeStruct((count, width), bf16),
            jax.ShapeDtypeStruct((MEM, width), bf16),
        ],
        in_specs=[anywhere, anywhere],
        out_specs=[anywhere, anywhere],
        scratch_shapes=[
            pltpu.VMEM((count, width), bf16),
            pltpu.VMEM((MEM, width), bf16),
            dma((2, 2, 2 * count // MEM)),
        ],
    )(*grads)
    return (grads[0][None, None], grads[1][None, None])


def solution(mesh):
    placed = (
        P(("groups", "seg"), None, "section"),
        P("section", ("groups", "seg"), None, None),
        P("section", ("groups", "seg"), None, None),
        P(("groups", "seg"), None, None),
        P("section", "seg", None),
        P("section", "seg", None),
        P("section", "seg", None),
        P("section", None),
        P("section", None, None),
        P("section", None),
    )
    sizes = (mesh.shape["seg"], mesh.shape["groups"], mesh.shape["section"])
    return jax.shard_map(
        functools.partial(per_device, *sizes),
        mesh=mesh,
        in_specs=placed,
        out_specs=(
            P("section", ("groups", "seg"), None, None),
            P("section", ("groups", "seg"), None, None),
        ),
        check_vma=False,
    )
```

```python
import functools

import jax
import jax.numpy as jnp
from jax import lax
from jax.experimental import pallas as pl
from jax.experimental.pallas import tpu as pltpu
from jax.sharding import PartitionSpec as P

HEADS = 16
KV_HEADS = 4
HEAD = 64
BLK = 128
MEM = 128


epsilon = 1e-05
masked_score = -1e30
GROUP = HEADS // KV_HEADS
NT = (((1,), (1,)), ((), ()))
TN = (((0,), (0,)), ((), ()))
CHUNKS = KV_HEADS
PAIR = 2
STRIPS = 4
KV, Q, O = 0, PAIR, PAIR + CHUNKS
PIECES = {KV: PAIR, Q: CHUNKS, O: STRIPS}
ITEMS = PAIR + CHUNKS + STRIPS
MESH = pl.DeviceIdType.MESH


def layer_kernel(
    n,
    groups,
    sections,
    pattern,
    writes,
    rows_far,
    up_far,
    gain,
    gate,
    gate_bias,
    w_kv,
    w_q,
    w_o,
    out_rows,
    out_memory,
    grad_rows,
    grad_memory,
    rows_in,
    ups,
    all_writes,
    all_kv,
    all_q,
    all_o,
    normed,
    scales,
    memory,
    state,
    passed,
    gates,
    keys,
    values,
    bias,
    dmixed,
    dmixed_out,
    dq,
    dkeys,
    dvalues,
    rowdots,
    *sems,
):
    (
        up_sem,
        down_sem,
        zrecv,
        xsend,
        xrecv,
        ysend,
        yrecv,
        wsend,
        wrecv,
        psend,
        precv,
        usend,
        urecv,
        dsend,
        drecv,
        local,
        leave,
    ) = sems
    g = lax.axis_index("groups")
    s = lax.axis_index("seg")
    c = lax.axis_index("section")
    count, width = rows_in.shape
    wide = writes.shape[1]
    span = all_q.shape[1] // CHUNKS
    half_kv = all_kv.shape[1] // PAIR
    f32, bf16 = jnp.float32, jnp.bfloat16
    native = n == CHUNKS

    owner = lax.rem(c, groups)
    owns = g == owner
    first, last = s == 0, s == n - 1
    end = first | last
    inner = jnp.logical_not(end)
    near_end = (s == 1) | (s == n - 2)
    far = jnp.where(s == 1, 0, n - 1)
    inward = jnp.where(first, 1, n - 2)

    def lanes(at, size):
        return pl.ds(pl.multiple_of(at * size, size), size)

    mine = lanes(c, wide)

    barrier = pltpu.get_barrier_semaphore()

    def greet(where):
        pl.semaphore_signal(barrier, inc=1, device_id=where, device_id_type=MESH)

    @pl.when(s > 0)
    def _():
        greet((g, s - 1, c))

    @pl.when(s < n - 1)
    def _():
        greet((g, s + 1, c))

    for d in range(1, groups):
        greet((lax.rem(g + d, groups), s, c))

        @pl.when(end)
        def _():
            greet((lax.rem(g + d, groups), inward, c))

        @pl.when(near_end)
        def _():
            greet((lax.rem(g + d, groups), far, c))

    for d in range(1, sections):
        greet((g, s, lax.rem(c + d, sections)))

    def input_copy(k):
        if k == 0:
            return pltpu.make_async_copy(rows_far, rows_in, local.at[3])
        return pltpu.make_async_copy(up_far, ups.at[g], local.at[4])

    input_copy(0).start()
    input_copy(1).start()

    beside = jnp.where(end, 1, 2) + jnp.where(end | near_end, groups - 1, 0)
    pl.semaphore_wait(barrier, beside + groups + sections - 2)

    def remote(src, dst, send, recv, where):
        return pltpu.make_async_remote_copy(
            src_ref=src,
            dst_ref=dst,
            send_sem=send,
            recv_sem=recv,
            device_id=where,
            device_id_type=MESH,
        )

    def operand(kind):
        return {
            KV: (w_kv, all_kv, half_kv),
            Q: (w_q, all_q, span),
            O: (w_o, all_o, width // STRIPS),
        }[kind]

    def columns(kind, chunk):
        cols = operand(kind)[2]
        if isinstance(chunk, int):
            return slice(chunk * cols, (chunk + 1) * cols)
        return lanes(chunk, cols)

    def spot(item, shard, part):
        kind, chunk = item
        src, dst, _ = operand(kind)
        at = columns(kind, chunk)
        if kind == O:
            return dst.at[lanes(shard, src.shape[0]), at]
        half = src.shape[0] // groups
        return dst.at[lanes(shard * groups + part, half), at]

    def source(item, part):
        kind, chunk = item
        src = operand(kind)[0]
        at = columns(kind, chunk)
        if kind == O:
            return src.at[:, at]
        return src.at[lanes(part, src.shape[0] // groups), at]

    def up(item, shard, own=False):
        i, there = item[0] + item[1], spot(item, shard, g)
        src = source(item, g) if own else there
        return remote(src, there, up_sem.at[i, shard], zrecv.at[i, shard], (g, s + 1, c))

    def down(item, shard, own=False):
        i, there = item[0] + item[1], spot(item, shard, g)
        src = source(item, g) if own else there
        return remote(src, there, down_sem.at[i, shard], zrecv.at[i, shard], (g, s - 1, c))

    def extra(j, d, shard, own=False):
        part = lax.rem(g + d, groups)
        there = spot((Q, j), shard, part)
        src = source((Q, j), part) if own else there
        return remote(src, there, xsend.at[j, d], xrecv.at[j, d], (g, inward, c))

    def across(item, shard, d, part):
        i, there = item[0] + item[1], spot(item, shard, part)
        return remote(
            there,
            there,
            ysend.at[i, shard, d],
            yrecv.at[i, shard, d],
            (lax.rem(g + d, groups), s, c),
        )

    def write_up(shard, own=False):
        there = all_writes.at[shard, :, mine]
        return remote(
            writes if own else there, there, wsend.at[shard], wrecv.at[shard], (g, s + 1, c)
        )

    def write_peer(shard, d, origin):
        there = all_writes.at[shard, :, lanes(origin, wide)]
        return remote(
            there,
            there,
            psend.at[shard, d],
            precv.at[shard, d],
            (g, s, lax.rem(c + d, sections)),
        )

    def pull_near():
        return remote(up_far, ups.at[g], usend.at[0], urecv.at[g], (owner, s, c))

    def pull_far():
        at = groups + g
        return remote(up_far, ups.at[at], usend.at[0], urecv.at[at], (owner, inward, c))

    def give_back(j, u, where):
        return remote(
            dmixed_out.at[j, u],
            dmixed.at[j],
            dsend.at[j, u],
            drecv.at[j],
            (lax.rem(u, groups), where, c),
        )

    def own_copy(w):
        src, dst = ((w_kv, all_kv), (w_o, all_o), (w_q, all_q))[w]
        return pltpu.make_async_copy(src, dst.at[lanes(s, src.shape[0]), :], local.at[w])

    def rises(kind):
        return (owns & (s > 0) & (s < n - 2)) | (owns & first) if kind == O else s < n - 1

    def falls(kind):
        return (owns & (s < n - 1) & (s > 1)) | (owns & last) if kind == O else s > 0

    def skips(kind, shard):
        if kind != Q:
            return shard < 0
        return ((shard == 0) & (s == 1)) | ((shard == n - 1) & (s == n - 2))

    def pieces(kind):
        return [(kind, k) for k in range(PIECES[kind])]

    rising = list(reversed(pieces(Q)))

    def start_own(kind):
        for fall in pieces(kind):
            rise = (kind, CHUNKS - 1 - fall[1]) if kind == Q else fall

            @pl.when(rises(kind))
            def _():
                up(rise, s, True).start()

            @pl.when(falls(kind))
            def _():
                down(fall, s, True).start()

    def spread(item, shard):
        if item[0] == O:
            return

        def send():
            for d in range(1, groups):
                across(item, shard, d, g).start()

        if item[0] == KV:
            send()
        else:
            pl.when(jnp.logical_not(skips(Q, shard)))(send)

    def from_below(item, shard):
        up(item, shard).wait_recv()

        @pl.when(rises(item[0]))
        def _():
            up(item, shard).start()

        spread(item, shard)

    def from_above(item, shard):
        down(item, shard).wait_recv()

        @pl.when(falls(item[0]))
        def _():
            down(item, shard).start()

        spread(item, shard)

    def reaches(kind):
        return owns & inner if kind == O else s >= 0

    def serve(kind, k, inside=False):
        low = 1 if inside else 0

        @pl.when((s - k >= low) & reaches(kind))
        def _():
            for item in rising if kind == Q else pieces(kind):
                from_below(item, s - k)

        @pl.when((s + k < n - low) & reaches(kind))
        def _():
            for item in pieces(kind):
                from_above(item, s + k)

    def finish(item):
        @pl.loop(0, n)
        def _(shard):
            skipped = skips(item[0], shard)

            @pl.when((shard != s) & jnp.logical_not(skipped))
            def _():
                for d in range(1, groups):
                    across(item, shard, d, lax.rem(g + groups - d, groups)).wait_recv()

            if item[0] == Q:

                @pl.when(skipped)
                def _():
                    for d in range(1, groups):
                        extra(item[1], d, shard).wait_recv()

    def drain(item):
        kind = item[0]

        @pl.loop(0, n)
        def _(shard):
            if kind != O:

                @pl.when((shard != s) & jnp.logical_not(skips(kind, shard)))
                def _():
                    for d in range(1, groups):
                        across(item, shard, d, g).wait_send()

            @pl.when((shard <= s) & rises(kind))
            def _():
                up(item, shard).wait_send()

            @pl.when((shard >= s) & falls(kind))
            def _():
                down(item, shard).wait_send()

    @pl.when(s < n - 1)
    def _():
        write_up(s, True).start()

    start_own(KV)

    @pl.when(inner & jnp.logical_not(owns))
    def _():
        pull_near().start()

    @pl.when(end & jnp.logical_not(owns))
    def _():
        pull_far().start()

    pl.when(first)(lambda: start_own(Q))
    start_own(O)
    pl.when(s > 0)(lambda: start_own(Q))

    @pl.when(end & owns)
    def _():
        pull_far().start()

    for w in range(3):
        own_copy(w).start()

    strip = 32

    def norm_rows(from_ref, to_row):
        @pl.loop(0, from_ref.shape[0] // strip)
        def _(r):
            x = from_ref[lanes(r, strip), :].astype(f32)
            scale = lax.rsqrt(jnp.mean(x * x, axis=-1, keepdims=True) + epsilon)
            to = pl.ds(pl.multiple_of(to_row + r * strip, strip), strip)
            normed[to, :] = (x * scale * gain[...]).astype(bf16)
            scales[to, :] = scale

    input_copy(0).wait()
    input_copy(1).wait()
    norm_rows(rows_in, MEM)

    whole_gate = gate[...]
    high = whole_gate.astype(bf16)
    rest = whole_gate - high.astype(f32)
    middle = rest.astype(bf16)
    gates[0] = high
    gates[1] = middle
    gates[2] = (rest - middle.astype(f32)).astype(bf16)

    keyed = lax.broadcasted_iota(jnp.int32, (BLK, BLK), 0)
    asked = lax.broadcasted_iota(jnp.int32, (BLK, BLK), 1)
    blocks = count // BLK
    for b in range(blocks):
        seen = jnp.where(pattern[b, 0] > 0, 0.0, masked_score)
        parts = [jnp.full((MEM, BLK), seen, f32)]
        for e in range(b):
            seen = jnp.where(pattern[b, 1 + e] > 0, 0.0, masked_score)
            parts.append(jnp.full((BLK, BLK), seen, f32))
        parts.append(jnp.where(keyed <= asked, 0.0, masked_score).astype(f32))
        for e, part in enumerate(parts):
            for r in range(PAIR):
                bias[b, e * BLK : (e + 1) * BLK, r * BLK : (r + 1) * BLK] = part

    state[...] = jnp.zeros_like(state)
    passed[...] = jnp.ones_like(passed)
    cut = width // HEADS

    def serve_writes(k):
        @pl.when(s - k >= 0)
        def _():
            write_up(s - k).wait_recv()

            @pl.when(s < n - 1)
            def _():
                write_up(s - k).start()

            for d in range(1, sections):
                write_peer(s - k, d, c).start()

    def add_writes(k):
        @pl.when(s - k >= 0)
        def _():
            for d in range(1, sections):
                write_peer(s - k, d, lax.rem(c + sections - d, sections)).wait_recv()
            w = all_writes[s - k]
            logits = sum(
                lax.dot_general(w, gates[p], NT, preferred_element_type=f32) for p in range(3)
            )
            keep = jax.nn.sigmoid(logits + gate_bias[...])
            fresh = passed[...] * (1.0 - keep)
            passed[...] = passed[...] * keep
            for h in range(HEADS):
                at = slice(h * cut, (h + 1) * cut)
                state[:, at] += fresh[:, h : h + 1] * w[:, at].astype(f32)

    def turn(t):
        return jnp.where(s < n // 2, t, CHUNKS - 1 - t)

    def sent_far(j):
        return (j != far) if native else (j >= 0)

    def give_all(t, away):
        j = turn(t)
        base = groups if away else 0
        weight = all_o[lanes(j, span), :]
        pulled = ups[base : base + groups].reshape(groups * count, width)
        part = lax.dot_general(pulled, weight, NT, preferred_element_type=f32).astype(bf16)
        for u in range(groups):
            piece = part[u * count : (u + 1) * count]
            dmixed_out[j, base + u] = piece
            if away:

                @pl.when(sent_far(j))
                def _():
                    give_back(j, base + u, far).start()

            else:

                @pl.when(u == g)
                def _():
                    dmixed[j] = piece

                @pl.when(u != g)
                def _():
                    give_back(j, u, s).start()

    def project(t):
        pl.when(owns & inner)(lambda: give_all(t, False))

    def project_far(t):
        pl.when(owns & near_end)(lambda: give_all(t, True))

    beyond = (lax.rem(g + 1, groups), s, c)

    def wait_pulls(low, high):
        @pl.loop(low, high)
        def _(u):
            @pl.when(u != g)
            def _():
                remote(up_far, ups.at[u], usend.at[0], urecv.at[u], beyond).wait_recv()

    def ready_near():
        @pl.when(owns & inner)
        def _():
            own_copy(1).wait()
            wait_pulls(0, groups)

    def ready_far():
        @pl.when(owns & near_end)
        def _():
            wait_pulls(groups, 2 * groups)

    def at(where, steps, among=None):
        who = s == where
        if among is not None:
            who = who & (owns if among else jnp.logical_not(owns))

        @pl.when(who)
        def _():
            for item, shard in steps:
                if shard < where:
                    from_below(item, shard)
                else:
                    from_above(item, shard)

    def all_of(items, *shards):
        return [(item, shard) for item in items for shard in shards]

    if n == 4:
        kvs, qs, os = pieces(KV), pieces(Q), pieces(O)
        serve_writes(1)
        at(0, all_of(kvs, 1))
        at(1, all_of(kvs, 2, 0))
        at(2, all_of(kvs, 3, 1))
        at(3, all_of(kvs, 2))
        add_writes(1)
        at(0, all_of(qs, 1))
        ups_0, downs_2, o_0, o_2 = (
            all_of(rising, 0),
            all_of(qs, 2),
            all_of(os, 0),
            all_of(os, 2),
        )
        at(
            1,
            o_2[:1]
            + ups_0[:2]
            + o_2[1:2]
            + ups_0[2:]
            + o_2[2:3]
            + o_0[:1]
            + o_2[3:]
            + downs_2[:3]
            + o_0[1:2]
            + downs_2[3:],
            True,
        )
        at(1, downs_2, False)
        ups_1, downs_3 = all_of(rising, 1), all_of(qs, 3)
        at(
            2,
            all_of(os, 3, 1)
            + downs_3[:1]
            + ups_1[:3]
            + downs_3[1:2]
            + ups_1[3:]
            + downs_3[2:3],
            True,
        )
        at(2, ups_1, False)
        at(3, all_of(rising, 2))
        serve_writes(2)
        at(0, all_of(kvs, 2))
        at(1, all_of(kvs, 3))
        at(1, o_0[2:3], True)
        at(2, downs_3[3:], True)
        at(2, all_of(kvs, 0))
        at(3, all_of(kvs, 1))
        add_writes(2)
        at(0, all_of(qs, 2) + all_of(kvs, 3))
        at(1, all_of(os, 3)[:1] + o_0[3:], True)
        mixed_steps = [step for pair in zip(ups_0, downs_3) for step in pair]
        at(1, mixed_steps, False)
        at(2, ups_0, True)
        at(2, downs_3[:3] + ups_0[:1] + downs_3[3:] + ups_0[1:], False)
        at(3, all_of(rising, 1))
        serve_writes(3)
        at(3, all_of(kvs, 0))
        @pl.when(end)
        def _():
            for j in range(CHUNKS):
                for d in range(1, groups):
                    extra(j, d, s, True).start()

        ready_near()
        for t in range(3):
            project(t)
        add_writes(3)
    else:

        @pl.loop(1, n)
        def _(k):
            serve_writes(k)
            serve(KV, k)
            serve(O, k)
            serve(Q, k, True)
            add_writes(k)

        @pl.when(end)
        def _():
            for j in range(CHUNKS):
                for d in range(1, groups):
                    extra(j, d, s, True).start()

        ready_near()
        for t in range(CHUNKS):
            project(t)
        ready_far()
        for t in range(CHUNKS):
            project_far(t)

        @pl.when(inner)
        def _():
            for fall, rise in zip(pieces(Q), rising):
                from_below(rise, 0)
                from_above(fall, n - 1)

    @pl.when(jnp.logical_not(owns & inner))
    def _():
        own_copy(1).wait()

        if native:

            @pl.when(end)
            def _():
                dmixed[s] = lax.dot_general(
                    ups[g], all_o[lanes(s, span), :], NT, preferred_element_type=f32
                ).astype(bf16)

    if n == 4:
        at(1, all_of(os, 3)[1:] + downs_3, True)

    memory[...] = state[...].astype(bf16)
    norm_rows(memory, 0)

    own_copy(0).wait()
    own_copy(2).wait()
    for item in pieces(KV):
        finish(item)
    for kind, to in ((0, keys), (1, values)):
        part = jnp.dot(
            normed[...], all_kv[:, kind * span : (kind + 1) * span], preferred_element_type=f32
        ).astype(bf16)
        for h in range(KV_HEADS):
            to[h] = part[:, h * HEAD : (h + 1) * HEAD]

    rowdots[...] = jnp.zeros_like(rowdots)

    if n == 4:
        at(2, o_0[:1], True)
        ready_far()
        project_far(1)
        project_far(2)
        at(2, o_0[1:], True)
        project(3)
        project_far(3)

    def attend(j):
        ready = owns & inner
        if native:
            ready = ready | (end & (j == s))

        @pl.when(jnp.logical_not(ready))
        def _():
            remote(
                dmixed_out.at[j, 0], dmixed.at[j], dsend.at[j, 0], drecv.at[j], beyond
            ).wait_recv()

        queries = jnp.dot(
            normed[MEM:, :], all_q[:, lanes(j, span)], preferred_element_type=f32
        ).astype(bf16)
        small = (queries.astype(f32) * HEAD ** (-0.5)).astype(bf16)
        key, value = keys[j], values[j]
        small_key = (key.astype(f32) * HEAD ** (-0.5)).astype(bf16)
        pulled = dmixed[j]
        dkey = [jnp.zeros((BLK, HEAD), f32) for _ in range(blocks + 1)]
        dvalue = [jnp.zeros((BLK, HEAD), f32) for _ in range(blocks + 1)]
        dquery = [[None] * blocks for _ in range(GROUP)]
        for h in range(0, GROUP, PAIR):
            for b in range(blocks):
                rows = slice(b * BLK, (b + 1) * BLK)
                depth = MEM + (b + 1) * BLK

                def stacked(x):
                    return jnp.concatenate(
                        [x[rows, (h + r) * HEAD : (h + r + 1) * HEAD] for r in range(PAIR)], axis=0
                    )

                query, dhead = stacked(small), stacked(pulled)
                scores = lax.dot_general(key[:depth], query, NT, preferred_element_type=f32)
                scores = scores + bias[b, :depth, :]
                raised = jnp.exp(scores - jnp.max(scores, axis=0, keepdims=True))
                probs = raised * (1.0 / jnp.sum(raised, axis=0, keepdims=True))
                dprobs = lax.dot_general(value[:depth], dhead, NT, preferred_element_type=f32)
                drop = jnp.sum(probs * dprobs, axis=0, keepdims=True)
                dscores = (probs * (dprobs - drop)).astype(bf16)
                dv = jnp.dot(probs.astype(bf16), dhead, preferred_element_type=f32)
                dk = jnp.dot(dscores, query, preferred_element_type=f32)
                for e in range(depth // BLK):
                    dvalue[e] += dv[e * BLK : (e + 1) * BLK]
                    dkey[e] += dk[e * BLK : (e + 1) * BLK]
                back = lax.dot_general(small_key[:depth], dscores, TN, preferred_element_type=f32)
                for r in range(PAIR):
                    dquery[h + r][b] = back[:, r * BLK : (r + 1) * BLK]
        dquery = [jnp.concatenate(parts, axis=1) for parts in dquery]
        dkey = jnp.concatenate(dkey, axis=0)
        dvalue = jnp.concatenate(dvalue, axis=0)
        dkey = dkey.astype(bf16)
        dvalue = dvalue.astype(bf16)
        dkeys[j] = dkey
        dvalues[j] = dvalue
        dquery = jnp.concatenate(dquery, axis=0).T.astype(bf16)
        dq[:, lanes(j, span)] = dquery
        rowdots[...] += jnp.sum(
            dkey.astype(f32) * key.astype(f32) + dvalue.astype(f32) * value.astype(f32),
            axis=-1,
            keepdims=True,
        )
        rowdots[MEM:, :] += jnp.sum(
            dquery.astype(f32) * queries.astype(f32), axis=-1, keepdims=True
        )

    def serve_end(t):
        j = turn(t)

        @pl.when(last)
        def _():
            from_below((Q, j), 0)

        @pl.when(first)
        def _():
            from_above((Q, j), n - 1)

    serve_end(0)
    serve_end(1)
    for t in range(CHUNKS):
        if t == 1:
            for later in range(2, CHUNKS):
                serve_end(later)
        j = turn(t)
        finish((Q, j))
        attend(j)

    dkv = jnp.concatenate(
        [dkeys[h] for h in range(KV_HEADS)] + [dvalues[h] for h in range(KV_HEADS)], axis=1
    )
    tile = 512
    scale = scales[...]
    coef = rowdots[...] * scale * scale * (1.0 / width)

    def leaving(t):
        at = lanes(t, tile)
        return (
            pltpu.make_async_copy(grad_rows.at[:, at], out_rows.at[:, at], leave.at[0, t]),
            pltpu.make_async_copy(grad_memory.at[:, at], out_memory.at[:, at], leave.at[1, t]),
        )

    @pl.loop(0, width // tile, unroll=4)
    def _(t):
        at = lanes(t, tile)
        both = lax.dot_general(dkv, all_kv[at, :], NT, preferred_element_type=f32)
        ones = lax.dot_general(dq[...], all_q[at, :], NT, preferred_element_type=f32)
        strength = gain[:, at]
        grad_memory[:, at] = (
            both[:MEM] * strength * scale[:MEM] - memory[:, at].astype(f32) * coef[:MEM]
        ).astype(bf16)
        grad_rows[:, at] = (
            (both[MEM:] + ones) * strength * scale[MEM:]
            - rows_in[:, at].astype(f32) * coef[MEM:]
            + ups[g, :, at].astype(f32)
        ).astype(bf16)
        for copy in leaving(t):
            copy.start()

    @pl.loop(0, n)
    def _(shard):
        @pl.when(shard < s)
        def _():
            for d in range(1, sections):
                write_peer(shard, d, c).wait_send()

        @pl.when((shard <= s) & (s < n - 1))
        def _():
            write_up(shard).wait_send()

    for kind in PIECES:
        for item in pieces(kind):
            drain(item)

    @pl.when(end)
    def _():
        pull_far().wait_send()
        for j in range(CHUNKS):
            for d in range(1, groups):
                extra(j, d, s, True).wait_send()

    @pl.when(inner & jnp.logical_not(owns))
    def _():
        pull_near().wait_send()

    @pl.loop(0, width // tile)
    def _(t):
        for copy in leaving(t):
            copy.wait()

    @pl.when(inner & owns)
    def _():
        @pl.loop(0, CHUNKS)
        def _(j):
            @pl.loop(0, 2 * groups)
            def _(u):
                @pl.when((u < groups) & (u != g))
                def _():
                    give_back(j, u, s).wait_send()

                @pl.when((u >= groups) & near_end & sent_far(j))
                def _():
                    give_back(j, u, far).wait_send()


def hand_over(rows_from, memory_from, rows_to, memory_to, rows, memory, sems):
    cut = memory_from.shape[0]

    def moves(k, src, dst, w, way):
        at = slice(k * cut, (k + 1) * cut)
        return pltpu.make_async_copy(src.at[at, :], dst.at[at, :], sems.at[way, w, k])

    pairs = ((rows_from, rows, rows_to), (memory_from, memory, memory_to))
    spans = [(w, k) for w in range(2) for k in range(pairs[w][0].shape[0] // cut)]
    for w, k in spans:
        moves(k, pairs[w][0], pairs[w][1], w, 0).start()
    for w, k in spans:
        moves(k, pairs[w][0], pairs[w][1], w, 0).wait()
        moves(k, pairs[w][1], pairs[w][2], w, 1).start()
    for w, k in spans:
        moves(k, pairs[w][1], pairs[w][2], w, 1).wait()


def per_device(
    n,
    groups,
    sections,
    writes,
    layer_inputs,
    upstream,
    pattern,
    w_q,
    w_kv,
    w_o,
    norm_gain,
    gate_weight,
    gate_bias,
):
    count, width = layer_inputs.shape[2:]
    total = MEM + count
    span = HEADS * HEAD // CHUNKS
    anywhere = pl.BlockSpec(memory_space=pl.ANY)
    near = pl.BlockSpec(memory_space=pltpu.VMEM)
    dma = pltpu.SemaphoreType.DMA
    bf16, f32 = jnp.bfloat16, jnp.float32
    grads = pl.pallas_call(
        functools.partial(layer_kernel, n, groups, sections),
        out_shape=[
            jax.ShapeDtypeStruct((count, width), bf16),
            jax.ShapeDtypeStruct((MEM, width), bf16),
        ],
        in_specs=[pl.BlockSpec(memory_space=pltpu.SMEM), anywhere, anywhere, anywhere]
        + [near] * 3
        + [anywhere] * 3,
        out_specs=[anywhere, anywhere],
        scratch_shapes=[
            pltpu.VMEM((count, width), bf16),
            pltpu.VMEM((MEM, width), bf16),
            pltpu.VMEM((count, width), bf16),
            pltpu.VMEM((2 * groups, count, width), bf16),
            pltpu.VMEM((n, MEM, width), bf16),
            pltpu.VMEM((width, w_kv.shape[2]), bf16),
            pltpu.VMEM((width, HEADS * HEAD), bf16),
            pltpu.VMEM((HEADS * HEAD, width), bf16),
            pltpu.VMEM((total, width), bf16),
            pltpu.VMEM((total, 1), f32),
            pltpu.VMEM((MEM, width), bf16),
            pltpu.VMEM((MEM, width), f32),
            pltpu.VMEM((MEM, HEADS), f32),
            pltpu.VMEM((3, HEADS, width), bf16),
            pltpu.VMEM((KV_HEADS, total, HEAD), bf16),
            pltpu.VMEM((KV_HEADS, total, HEAD), bf16),
            pltpu.VMEM((count // BLK, total, PAIR * BLK), f32),
            pltpu.VMEM((KV_HEADS, count, span), bf16),
            pltpu.VMEM((KV_HEADS, 2 * groups, count, span), bf16),
            pltpu.VMEM((count, HEADS * HEAD), bf16),
            pltpu.VMEM((KV_HEADS, total, HEAD), bf16),
            pltpu.VMEM((KV_HEADS, total, HEAD), bf16),
            pltpu.VMEM((total, 1), f32),
            dma((ITEMS, n)),
            dma((ITEMS, n)),
            dma((ITEMS, n)),
            dma((CHUNKS, groups)),
            dma((CHUNKS, groups)),
            dma((O, n, groups)),
            dma((O, n, groups)),
            dma((n,)),
            dma((n,)),
            dma((n, sections)),
            dma((n, sections)),
            dma((1,)),
            dma((2 * groups,)),
            dma((CHUNKS, 2 * groups)),
            dma((CHUNKS,)),
            dma((5,)),
            dma((2, width // 512)),
        ],
        compiler_params=pltpu.CompilerParams(
            collective_id=0, has_side_effects=True, vmem_limit_bytes=56 * 1024 * 1024
        ),
    )(
        pattern[0],
        writes[0],
        layer_inputs[0, 0],
        upstream[0, 0],
        norm_gain,
        gate_weight[0].T,
        gate_bias,
        w_kv[0],
        w_q[0],
        w_o[0],
    )
    grads = pl.pallas_call(
        hand_over,
        out_shape=[
            jax.ShapeDtypeStruct((count, width), bf16),
            jax.ShapeDtypeStruct((MEM, width), bf16),
        ],
        in_specs=[anywhere, anywhere],
        out_specs=[anywhere, anywhere],
        scratch_shapes=[
            pltpu.VMEM((count, width), bf16),
            pltpu.VMEM((MEM, width), bf16),
            dma((2, 2, count // MEM)),
        ],
    )(*grads)
    return (grads[0][None, None], grads[1][None, None])


def solution(mesh):
    placed = (
        P(("groups", "seg"), None, "section"),
        P("section", ("groups", "seg"), None, None),
        P("section", ("groups", "seg"), None, None),
        P(("groups", "seg"), None, None),
        P("section", "seg", None),
        P("section", "seg", None),
        P("section", "seg", None),
        P("section", None),
        P("section", None, None),
        P("section", None),
    )
    sizes = (mesh.shape["seg"], mesh.shape["groups"], mesh.shape["section"])
    return jax.shard_map(
        functools.partial(per_device, *sizes),
        mesh=mesh,
        in_specs=placed,
        out_specs=(
            P("section", ("groups", "seg"), None, None),
            P("section", ("groups", "seg"), None, None),
        ),
        check_vma=False,
    )
```
